32 devices in a mesh: layer: 8 (over z, x), batch: 4 (over y, core).
Axes of the slice: x: 2, y: 2, z: 4, core: 2. Of those that a mesh axis runs over, the one named last changes fastest.
Arguments:
- inputs: float32 [4, 8, 8, 8, 128], P('batch'), parts along dimension 0, may hold values from -6 to 6
- guess_states: float32 [32, 4, 8, 8, 8, 128], P('layer', 'batch'), parts along dimension 1, may hold values from -6 to 6
- kernels: bfloat16 [32, 3, 3, 3, 128, 128], P('layer'), may hold values from -0.109375 to 0.109375
- biases: float32 [32, 128], P('layer'), may hold values from -4 to 4
Outputs:
- states: float32 [32, 4, 8, 8, 8, 128], P('layer', 'batch'), parts along dimension 1
- coarse_residual: float32 [8, 4, 8, 8, 8, 128], P('layer', 'batch'), parts along dimension 1
The draws below stay inside these ranges and needn't reach their ends.
There are 4 independent parts, one for each index of `batch`. The reference program is written for one: setup_inputs(seed, part) draws one part's arguments, and reference() takes and returns one part's arrays. A program takes and returns all parts, laid end to end along the dimension named above; an argument that names none is the same for every part. Nothing has to cross between parts.
All inputs are finite; a program needn't handle non-finite values.
Results may differ from the reference program's by a relative error of at most 0.0008.
Values may be sent and summed in bfloat16 or wider, within the bound.
A program may use at most 128 MiB of HBM per device.

```python
import jax
import jax.numpy as jnp
from jax import lax

CHANNELS = 128
VX = 8
VY = 8
VZ = 8
CLIPS = 1
SECT = 4
COARSEN = 4
LAYERS = 32
N_LAYER = 8


def level_of(stream_key, shape, cuts, low, high):
    def one(dim, blocks):
        steps = jax.random.uniform(jax.random.fold_in(jax.random.fold_in(stream_key, 6), dim), (blocks,), jnp.float32, low / len(cuts), high / len(cuts))
        return jnp.repeat(jnp.exp(steps), shape[dim] // blocks).reshape((-1,) + (1,) * (len(shape) - dim - 1))

    level = one(*cuts[0])
    for cut in cuts[1:]:
        level = level * one(*cut)
    return level


def bell_draw(stream_key, extent, scale, bound, shards=(), held_as=jnp.bfloat16):
    drawn = jax.random.normal(stream_key, extent, jnp.float32) * scale
    if len(shards) > 0:
        drawn = level_of(stream_key, extent, shards, -0.22, 0.18) * drawn
    return jnp.clip(drawn, min=-bound, max=bound).astype(held_as)


def setup_inputs(seed: int = 0, part: int = 0) -> dict:
    key_list = jax.random.split(jax.random.key(seed), 5)
    part_keys = jax.random.split(jax.random.fold_in(key_list[4], part), 5)
    inputs = bell_draw(part_keys[0], (CLIPS, VX, VY, VZ, CHANNELS), 1.0, 6.0, (), jnp.float32)
    guess_states = bell_draw(part_keys[1], (LAYERS, CLIPS, VX, VY, VZ, CHANNELS), 1.0, 6.0, ((0, 8),), jnp.float32)
    kernels = bell_draw(key_list[2], (LAYERS, 3, 3, 3, CHANNELS, CHANNELS), (27 * CHANNELS) ** -0.5, 0.109375, ((0, 8),))
    biases = bell_draw(key_list[3], (LAYERS, CHANNELS), 1.0, 4.0, ((0, 8),), jnp.float32)
    return dict(inputs=inputs, guess_states=guess_states, kernels=kernels, biases=biases)


def advance(state, kernel, offset_row, step_size):
    squashed = lax.optimization_barrier(jnp.tanh(state).astype(jnp.bfloat16)).astype(jnp.float32)
    count, size_x, size_y, size_z, width = state.shape
    padded = jnp.pad(squashed, ((0, 0), (1, 1), (1, 1), (1, 1), (0, 0)))
    pieces = []
    for shift_a in range(3):
        for shift_b in range(3):
            for shift_d in range(3):
                pieces.append(padded[:, shift_a:shift_a + size_x, shift_b:shift_b + size_y, shift_d:shift_d + size_z, :])
    columns = jnp.concatenate(pieces, -1).reshape((-1, 27 * width))
    matrix = kernel.astype(jnp.float32).reshape((27 * width, kernel.shape[-1]))
    mixed = jnp.dot(columns, matrix, precision=lax.Precision.HIGHEST, preferred_element_type=jnp.float32)
    mixed = mixed.reshape((count, size_x, size_y, size_z, kernel.shape[-1]))
    return state + step_size * (mixed + offset_row)


def reference(inputs, guess_states, kernels, biases):
    sections = N_LAYER
    depth = SECT
    groups = sections // COARSEN
    fine_size = 2.0 / (SECT * N_LAYER)
    coarse_size = depth * fine_size
    top_size = COARSEN * coarse_size
    stepper = jax.vmap(advance, in_axes=(0, 0, 0, None))
    tail = guess_states.shape[1:]
    states = guess_states.reshape((sections, depth) + tail)
    kernel_grid = kernels.reshape((sections, depth) + kernels.shape[1:])
    bias_grid = biases.reshape((sections, depth, biases.shape[-1]))

    def heads_of(current):
        return jnp.concatenate([inputs[None], current[:-1, -1]], 0)

    def relax_fine(current):
        chain_rows = [heads_of(current)]
        for layer_row in range(1, depth):
            chain_rows.append(stepper(chain_rows[-1], kernel_grid[:, layer_row - 1], bias_grid[:, layer_row - 1], fine_size))
        return jnp.stack(chain_rows[1:] + [current[:, -1]], 1)

    def settle_fine(current):
        corner = stepper(current[:, -2], kernel_grid[:, -1], bias_grid[:, -1], fine_size)
        return current.at[:, -1].set(corner)

    states = relax_fine(settle_fine(relax_fine(states)))
    heads = heads_of(states)
    fine_defect = stepper(states[:, -2], kernel_grid[:, -1], bias_grid[:, -1], fine_size) - stepper(heads, kernel_grid[:, 0], bias_grid[:, 0], coarse_size)

    coarse_values = states[:, -1].reshape((groups, COARSEN) + tail)
    coarse_defect = fine_defect.reshape((groups, COARSEN) + tail)
    coarse_kernels = kernel_grid[:, 0].reshape((groups, COARSEN) + kernels.shape[1:])
    coarse_biases = bias_grid[:, 0].reshape((groups, COARSEN, biases.shape[-1]))

    def coarse_heads(current):
        return jnp.concatenate([inputs[None], current[:-1, -1]], 0)

    def relax_coarse(current):
        chain_rows = [coarse_heads(current)]
        for turn in range(COARSEN - 1):
            chain_rows.append(stepper(chain_rows[-1], coarse_kernels[:, turn], coarse_biases[:, turn], coarse_size) + coarse_defect[:, turn])
        return jnp.stack(chain_rows[1:] + [current[:, -1]], 1)

    def settle_coarse(current):
        corner = stepper(current[:, -2], coarse_kernels[:, -1], coarse_biases[:, -1], coarse_size) + coarse_defect[:, -1]
        return current.at[:, -1].set(corner)

    coarse_values = relax_coarse(settle_coarse(relax_coarse(coarse_values)))
    group_heads = coarse_heads(coarse_values)
    flat_values = coarse_values.reshape((sections,) + tail)
    flat_heads = jnp.concatenate([inputs[None], flat_values[:-1]], 0)
    corner_all = stepper(flat_heads, kernel_grid[:, 0], bias_grid[:, 0], coarse_size) + fine_defect
    coarse_residual = corner_all - flat_values
    corner_owner = corner_all.reshape((groups, COARSEN) + tail)[:, -1]
    level_defect = corner_owner - stepper(group_heads, coarse_kernels[:, -1], coarse_biases[:, -1], top_size)

    level_two = inputs
    solved = []
    for turn in range(groups):
        level_two = advance(level_two, coarse_kernels[turn, -1], coarse_biases[turn, -1], top_size) + level_defect[turn]
        solved.append(level_two)
    coarse_values = coarse_values.at[:, -1].set(jnp.stack(solved, 0))
    coarse_values = relax_coarse(coarse_values)

    states = states.at[:, -1].set(coarse_values.reshape((sections,) + tail))
    states = relax_fine(states)
    return states.reshape(guess_states.shape), coarse_residual
```

```python
import jax
import jax.numpy as jnp
from jax import lax
from jax.experimental import pallas as pl
from jax.experimental.pallas import tpu as pltpu
from jax.sharding import PartitionSpec as P

COARSEN = 4
TAPS = 3
MESH = pl.DeviceIdType.MESH


def cycle_kernel(sections, inputs_hbm, guess_ref, kern_ref, bias_hbm, states_ref, residual_ref,
                 inputs_ref, bias_ref, fine_w, lead_w, patches, cur, head, head_mix,
                 first_head, next_head, corner_out, seed_out, seed_in, c_point,
                 start_in, top_in, top_out, defects,
                 load_sem, small_sem, hop_send, hop_recv, w_send, w_recv, relay_send, sib_send, sib_recv,
                 g_send, g_recv, seed_send, seed_recv, start_send, start_recv, top_send, top_recv):
    depth = guess_ref.shape[0]
    size_x, size_y, size_z, width = inputs_ref.shape
    groups = sections // COARSEN
    fine_size = 2.0 / (depth * sections)
    coarse_size = depth * fine_size
    top_size = COARSEN * coarse_size
    rows = TAPS * TAPS * width
    half_rows = rows // 2
    last = COARSEN - 1
    me = lax.axis_index("layer")
    part = lax.axis_index("batch")
    pos = lax.rem(me, COARSEN)
    group = me // COARSEN
    core = lax.rem(part, 2)
    sibling = part + 1 - 2 * core
    both = jnp.logical_and
    is_first = me == 0
    has_next = me < sections - 1
    later = group > 0
    has_group_after = group < groups - 1
    is_last_pos = pos == last

    def device(p, ahead=0):
        return ((group + ahead) * COARSEN + p, part)

    barrier = pltpu.get_barrier_semaphore()

    def greet(target):
        pl.semaphore_signal(barrier, inc=1, device_id=target, device_id_type=MESH)

    for rel in range(1, COARSEN):
        greet(device(lax.rem(pos + rel, COARSEN)))
    greet((me, sibling))
    sends_ahead = both(is_last_pos, has_group_after)

    @pl.when(sends_ahead)
    def _():
        for p in range(COARSEN):
            greet(device(p, 1))

    pl.when(later)(lambda: greet(device(last, -1)))

    def fine_load(layer, tap):
        return pltpu.make_async_copy(
            kern_ref.at[layer, tap],
            fine_w.at[layer, :, pl.ds(tap * width, width)],
            load_sem.at[layer, tap],
        )

    inputs_load = pltpu.make_async_copy(inputs_hbm, inputs_ref, small_sem.at[0])
    bias_load = pltpu.make_async_copy(bias_hbm, bias_ref, small_sem.at[1])
    inputs_load.start()
    bias_load.start()
    for layer in range(depth):
        for tap in range(TAPS):
            fine_load(layer, tap).start()

    pl.semaphore_wait(barrier, COARSEN + jnp.where(sends_ahead, COARSEN, 0) + jnp.where(later, 1, 0))

    def remote(source, target, send_sem, recv_sem, where):
        return pltpu.make_async_remote_copy(
            src_ref=source, dst_ref=target, send_sem=send_sem, recv_sem=recv_sem,
            device_id=where, device_id_type=MESH)

    def hop(index, source, target):
        return remote(source, target, hop_send.at[index], hop_recv.at[index], (me + 1, part))

    first_hop = hop(0, guess_ref.at[depth - 1, 0], first_head)
    second_hop = hop(1, corner_out, next_head)
    pl.when(has_next)(first_hop.start)

    half = pl.ds(pl.multiple_of(core * half_rows, 16), half_rows)
    slot = jnp.minimum(pos, last - 1)

    def column(tap):
        return pl.ds(tap * width, width)

    def gives_w(p):
        direct = both(pos < p, jnp.logical_or(later, pos == last - 1))
        return both(direct, pos != 0) if p == last else direct

    def takes(q):
        return both(pos > q, jnp.logical_or(later, q == last - 1))

    def w_copy(p, tap):
        return remote(kern_ref.at[0, tap, half], lead_w.at[slot, half, column(tap)],
                      w_send.at[p, tap], w_recv.at[slot, tap], device(p))

    def w_arrival(q, tap):
        return remote(lead_w.at[q, half, column(tap)], lead_w.at[q, half, column(tap)],
                      w_send.at[0, tap], w_recv.at[q, tap], device(q))

    def relay(tap):
        return remote(lead_w.at[0, half, column(tap)], lead_w.at[0, half, column(tap)],
                      relay_send.at[tap], w_recv.at[0, tap], device(last))

    def sib_copy(q):
        return remote(lead_w.at[q, half], lead_w.at[q, half], sib_send.at[q], sib_recv.at[q], (me, sibling))

    def send_w(taps):
        for tap in taps:
            for p in range(last, 0, -1):
                pl.when(gives_w(p))(w_copy(p, tap).start)

    relays = both(pos == 1, later)

    def send_relay(taps):
        @pl.when(relays)
        def _():
            for tap in taps:
                w_arrival(0, tap).wait_recv()
                relay(tap).start()

    def settle_w(q):
        for tap in range(TAPS):
            arrives = pos != 1 if q == 0 else True
            pl.when(arrives)(w_arrival(q, tap).wait_recv)
        sib_copy(q).start()

    send_w(range(TAPS - 1))

    z_index = lax.broadcasted_iota(jnp.int32, (size_x * size_y, size_z, width), 1)

    def mix(state, weights):
        squashed = jnp.tanh(state).reshape(size_x * size_y, size_z, width)
        below = jnp.where(z_index == 0, 0.0, pltpu.roll(squashed, 1, 1))
        above = jnp.where(z_index == size_z - 1, 0.0, pltpu.roll(squashed, size_z - 1, 1))
        span = size_y * size_z
        edge = jnp.zeros((size_x, size_z, width), jnp.float32)
        for tap_z, shifted in enumerate((below, squashed, above)):
            shifted = shifted.reshape(size_x, span, width)
            even = shifted.astype(jnp.bfloat16)
            odd = jnp.concatenate([edge, shifted, edge], 1).astype(jnp.bfloat16)
            for tap_y, block in enumerate((odd[:, :span], even, odd[:, 2 * size_z:])):
                column = (tap_y * TAPS + tap_z) * width
                patches[:, :, column:column + width] = block
        left = patches[...].reshape(size_x * span, rows)
        product = jnp.dot(left, weights[...], preferred_element_type=jnp.float32)
        product = product.reshape(size_x, size_y, size_z, TAPS * width)
        plane = jnp.zeros((1, size_y, size_z, width), jnp.float32)
        total = product[..., width:2 * width]
        total = total + jnp.concatenate([plane, product[:-1, :, :, :width]], 0)
        return total + jnp.concatenate([product[1:, :, :, 2 * width:], plane], 0)

    def fine_step(layer):
        state = cur[...]
        mixed = mix(state, fine_w.at[layer])
        return state, mixed, state + fine_size * (mixed + bias_ref[layer])

    pl.when(me > 0)(first_hop.wait_recv)
    inputs_load.wait()
    bias_load.wait()
    cur[...] = jnp.where(is_first, inputs_ref[...], first_head[...])

    for layer in range(depth):
        for tap in range(TAPS):
            fine_load(layer, tap).wait()

    def sweep_one(layer, carry):
        after = fine_step(layer)[2]
        cur[...] = after
        states_ref[layer, 0] = after
        return carry

    lax.fori_loop(0, depth, sweep_one, 0)
    corner_out[...] = cur[...]
    pl.when(has_next)(second_hop.start)
    send_w(range(TAPS - 1, TAPS))

    def seed_copy(p):
        return remote(seed_out, seed_in, seed_send.at[p], seed_recv, device(p))

    def gives_seed(p):
        first_group = both(group == 0, pos == 1) if p >= 2 else False
        return jnp.logical_or(first_group, both(later, pos == 0)) if p == last else first_group

    takes_seed = jnp.logical_or(is_last_pos, both(group == 0, pos == 2))

    def g_copy(p):
        return remote(defects.at[pos], defects.at[pos], g_send.at[p], g_recv.at[slot], device(p))

    def g_arrival(q):
        return remote(defects.at[q], defects.at[q], g_send.at[0], g_recv.at[q], device(q))

    def gives_g(p):
        return both(pos < p, jnp.logical_or(later, pos == last - 1))

    @pl.when(me > 0)
    def _():
        second_hop.wait_recv()
        send_relay(range(TAPS - 1))
        head[...] = next_head[...]
        cur[...] = next_head[...]

        def sweep_two(layer, carry):
            _, mixed, after = fine_step(layer)

            @pl.when(layer == 0)
            def _():
                head_mix[...] = mixed

            cur[...] = after
            states_ref[layer, 0] = after
            return carry

        lax.fori_loop(0, depth, sweep_two, 0)
        seed_out[...] = cur[...]
        for p in range(2, COARSEN):
            pl.when(gives_seed(p))(seed_copy(p).start)
        defects[pos] = cur[...] - head[...] - coarse_size * head_mix[...]
        for p in (last, 1, 2):
            pl.when(gives_g(p))(g_copy(p).start)
        send_relay(range(TAPS - 1, TAPS))

    def exchange(qs):
        for q in qs:
            @pl.when(takes(q))
            def _(q=q):
                settle_w(q)
        for q in qs:
            pl.when(takes(q))(sib_copy(q).wait_recv)

    def own_step():
        state = cur[...]
        mixed = mix(state, fine_w.at[0])
        head[...] = state
        head_mix[...] = mixed
        return state + coarse_size * mixed + defects[pos]

    def chain(low, high, arriving=False):
        def step(turn, carry):
            state = cur[...]
            mixed = mix(state, lead_w.at[turn])
            if arriving:
                g_arrival(turn).wait_recv()
            cur[...] = state + coarse_size * mixed + defects[turn]
            return carry

        lax.fori_loop(low, high, step, 0)

    def top_copy(p):
        return remote(top_out, top_in, top_send.at[p], top_recv, device(p, 1))

    def send_top():
        for p in range(last, -1, -1):
            top_copy(p).start()

    start_copy = remote(c_point, start_in, start_send, start_recv, device(last, 1))

    pl.when(takes_seed)(seed_copy(0).wait_recv)

    @pl.when(is_last_pos)
    def _():
        exchange(range(1, last))
        cur[...] = seed_in[...]
        chain(jnp.where(later, 1, 2), last, arriving=True)
        relaxed = own_step()
        c_point[...] = relaxed
        top_out[...] = relaxed
        states_ref[last, 0] = relaxed
        pl.when(both(group == 0, has_group_after))(send_top)
        pl.when(both(later, has_group_after))(start_copy.start)
        exchange(range(1))

    @pl.when(jnp.logical_not(is_last_pos))
    def _():
        exchange(range(last - 1))

    for q in range(last):
        waits = both(takes(q), jnp.logical_not(is_last_pos)) if q > 0 else takes(q)
        pl.when(waits)(g_arrival(q).wait_recv)

    has_start = both(is_last_pos, group > 1)

    @pl.when(has_start)
    def _():
        start_copy.wait_recv()
        cur[...] = start_in[...]
        chain(0, last)
        corner = own_step()
        residual_ref[0, 0] = corner - c_point[...]
        start = start_in[...]
        top_rhs = corner - start - top_size * mix(start, fine_w.at[0])
        top_out[...] = top_rhs

    @pl.when(later)
    def _():
        top_copy(0).wait_recv()

    @pl.when(has_start)
    def _():
        solved = top_in[...]
        top_out[...] = solved + top_size * mix(solved, fine_w.at[0]) + top_out[...]
        pl.when(has_group_after)(send_top)

    steps = jnp.logical_or(later, pos == 2)

    @pl.when(steps)
    def _():
        cur[...] = jnp.where(later, top_in[...], seed_in[...])
        chain(0, jnp.where(later, pos, 0))
        after = own_step()
        states_ref[last, 0] = jnp.where(has_start, top_out[...], after)

        @pl.when(jnp.logical_not(has_start))
        def _():
            residual_ref[0, 0] = after - jnp.where(is_last_pos, c_point[...], after)

        @pl.when(both(is_last_pos, group == 1))
        def _():
            top_out[...] = after
            pl.when(has_group_after)(send_top)

    @pl.when(jnp.logical_not(steps))
    def _():
        corner = states_ref[last, 0]
        residual_ref[0, 0] = corner - corner

    @pl.when(me > 1)
    def _():
        cur[...] = head[...] + fine_size * (head_mix[...] + bias_ref[0])
        states_ref[0, 0] = cur[...]

        def last_sweep(layer, carry):
            after = fine_step(layer)[2]
            cur[...] = after
            states_ref[layer, 0] = after
            return carry

        lax.fori_loop(1, depth - 1, last_sweep, 0)

    pl.when(has_next)(first_hop.wait_send)
    pl.when(has_next)(second_hop.wait_send)
    for p in range(1, COARSEN):
        @pl.when(gives_w(p))
        def _(p=p):
            for tap in range(TAPS):
                w_copy(p, tap).wait_send()

        pl.when(gives_g(p))(g_copy(p).wait_send)
        if p > 1:
            pl.when(gives_seed(p))(seed_copy(p).wait_send)
    for q in range(last):
        pl.when(takes(q))(sib_copy(q).wait_send)

    @pl.when(relays)
    def _():
        for tap in range(TAPS):
            relay(tap).wait_send()

    @pl.when(sends_ahead)
    def _():
        for p in range(COARSEN):
            top_copy(p).wait_send()
        pl.when(later)(start_copy.wait_send)


def shards(inputs, guess_states, kernels, biases):
    sections = lax.axis_size("layer")
    depth = guess_states.shape[0]
    state = inputs.shape[1:]
    width = state[-1]
    rows = TAPS * TAPS * width
    vmem = pl.BlockSpec(memory_space=pltpu.VMEM)
    hbm = pl.BlockSpec(memory_space=pltpu.HBM)
    kernel_rows = kernels.reshape(depth, TAPS, rows, width)
    bias_rows = biases.reshape(depth, 1, 1, width)
    f32_state = pltpu.VMEM(state, jnp.float32)
    dma = pltpu.SemaphoreType.DMA
    operands = [pltpu.with_memory_space_constraint(operand, pltpu.HBM)
                for operand in (inputs.reshape(state), guess_states, kernel_rows, bias_rows)]

    def body(*refs):
        cycle_kernel(sections, *refs)

    return tuple(pl.pallas_call(
        body,
        name="mgrit_cycle",
        out_shape=(
            pltpu.VMEM(guess_states.shape, jnp.float32),
            pltpu.VMEM((1,) + guess_states.shape[1:], jnp.float32),
        ),
        in_specs=[hbm, hbm, hbm, hbm],
        out_specs=(vmem, vmem),
        scratch_shapes=[
            f32_state, pltpu.VMEM(bias_rows.shape, jnp.float32),
            pltpu.VMEM((depth, rows, TAPS * width), jnp.bfloat16),
            pltpu.VMEM((COARSEN - 1, rows, TAPS * width), jnp.bfloat16),
            pltpu.VMEM((state[0], state[1] * state[2], rows), jnp.bfloat16),
            f32_state, f32_state, f32_state, f32_state, f32_state, f32_state,
            f32_state, f32_state, f32_state, f32_state, f32_state, f32_state,
            pltpu.VMEM((COARSEN,) + state, jnp.float32),
            dma((depth, TAPS)), dma((2,)), dma((2,)), dma((2,)),
            dma((COARSEN, TAPS)), dma((COARSEN - 1, TAPS)), dma((TAPS,)),
            dma((COARSEN - 1,)), dma((COARSEN - 1,)),
            dma((COARSEN,)), dma((COARSEN - 1,)), dma((COARSEN,)), dma, dma, dma, dma((COARSEN,)), dma,
        ],
        compiler_params=pltpu.CompilerParams(
            collective_id=0, has_side_effects=True, vmem_limit_bytes=24 * 1024 * 1024),
    )(*operands))


def solution(mesh):
    return jax.shard_map(
        shards,
        mesh=mesh,
        in_specs=(
            P("batch", None, None, None, None),
            P("layer", "batch", None, None, None, None),
            P("layer", None, None, None, None, None),
            P("layer", None),
        ),
        out_specs=(
            P("layer", "batch", None, None, None, None),
            P("layer", "batch", None, None, None, None),
        ),
        check_vma=False,
    )
```

```python
import jax
import jax.numpy as jnp
from jax import lax
from jax.experimental import pallas as pl
from jax.experimental.pallas import tpu as pltpu
from jax.sharding import PartitionSpec as P

COARSEN = 4
TAPS = 3
PIECES = 4
MESH = pl.DeviceIdType.MESH


def cycle_kernel(sections, inputs_hbm, guess_ref, kern_ref, bias_hbm, states_ref, residual_ref,
                 inputs_ref, bias_ref, fine_w, lead_w, patches, cur, head, head_mix,
                 first_head, next_head, corner_out, seed_out, seed_in, c_point,
                 start_in, top_in, top_out, defects,
                 load_sem, small_sem, hop_send, hop_recv, w_send, w_recv, y_send, y_recv, sib_send, sib_recv,
                 extra_send, extra_recv,
                 g_send, g_recv, seed_send, seed_recv, start_send, start_recv, top_send, top_recv):
    depth = guess_ref.shape[0]
    size_x, size_y, size_z, width = inputs_ref.shape
    groups = sections // COARSEN
    fine_size = 2.0 / (depth * sections)
    coarse_size = depth * fine_size
    top_size = COARSEN * coarse_size
    rows = TAPS * TAPS * width
    piece_rows = rows // PIECES
    last = COARSEN - 1
    extra = COARSEN - 2
    me = lax.axis_index("layer")
    part = lax.axis_index("batch")
    pos = lax.rem(me, COARSEN)
    group = me // COARSEN
    core = lax.rem(part, 2)
    row = lax.rem(part // 2, 2)
    sibling = part + 1 - 2 * core
    across = part + 2 - 4 * row
    both = jnp.logical_and
    either = jnp.logical_or
    is_first = me == 0
    has_next = me < sections - 1
    later = group > 0
    opening = group == 0
    has_group_after = group < groups - 1
    is_last_pos = pos == last
    is_upper = pos >= last - 1

    def device(p, ahead=0):
        return ((group + ahead) * COARSEN + p, part)

    barrier = pltpu.get_barrier_semaphore()

    def greet(target):
        pl.semaphore_signal(barrier, inc=1, device_id=target, device_id_type=MESH)

    for rel in range(1, COARSEN):
        greet(device(lax.rem(pos + rel, COARSEN)))
    greet((me, sibling))
    greet((me, across))
    greets_ahead = both(is_upper, has_group_after)

    @pl.when(greets_ahead)
    def _():
        for p in range(COARSEN):
            greet(device(p, 1))

    @pl.when(later)
    def _():
        for p in (last - 1, last):
            greet(device(p, -1))

    def fine_load(layer, tap):
        return pltpu.make_async_copy(
            kern_ref.at[layer, tap],
            fine_w.at[layer, :, pl.ds(tap * width, width)],
            load_sem.at[layer, tap],
        )

    inputs_load = pltpu.make_async_copy(inputs_hbm, inputs_ref, small_sem.at[0])
    bias_load = pltpu.make_async_copy(bias_hbm, bias_ref, small_sem.at[1])
    inputs_load.start()
    bias_load.start()
    for layer in range(depth):
        for tap in range(TAPS):
            fine_load(layer, tap).start()

    greetings = COARSEN + 1 + jnp.where(greets_ahead, COARSEN, 0) + jnp.where(later, 2, 0)
    pl.semaphore_wait(barrier, greetings)

    def remote(source, target, send_sem, recv_sem, where):
        return pltpu.make_async_remote_copy(
            src_ref=source, dst_ref=target, send_sem=send_sem, recv_sem=recv_sem,
            device_id=where, device_id_type=MESH)

    def hop(index, source, target):
        return remote(source, target, hop_send.at[index], hop_recv.at[index], (me + 1, part))

    first_hop = hop(0, guess_ref.at[depth - 1, 0], first_head)
    second_hop = hop(1, corner_out, next_head)
    pl.when(has_next)(first_hop.start)

    slot = jnp.minimum(pos, last - 1)
    quarter = pl.ds(pl.multiple_of((core * 2 + row) * piece_rows, 16), piece_rows)
    half = pl.ds(pl.multiple_of(core * 2 * piece_rows, 16), 2 * piece_rows)

    def w_copy(p):
        return remote(fine_w.at[0, quarter], lead_w.at[slot, quarter], w_send.at[p], w_recv.at[slot], device(p))

    def w_arrival(q):
        return remote(lead_w.at[q, quarter], lead_w.at[q, quarter], w_send.at[0], w_recv.at[q], device(q))

    def y_copy(q):
        return remote(lead_w.at[q, quarter], lead_w.at[q, quarter], y_send.at[q], y_recv.at[q], (me, across))

    def sib_copy(q):
        return remote(lead_w.at[q, half], lead_w.at[q, half], sib_send.at[q], sib_recv.at[q], (me, sibling))

    def extra_copy(index):
        piece = pl.ds(index * piece_rows, piece_rows)
        return remote(fine_w.at[0, piece], lead_w.at[extra, piece], extra_send.at[index], extra_recv.at[index],
                      device(2 * last - 1 - pos))

    gives_extra = both(opening, either(both(pos == last - 1, core == 0), both(pos == last, core == 1)))
    finishes = both(opening, either(both(pos == last, core == 0), both(pos == last - 1, core == 1)))

    def send_w(source, targets):
        @pl.when(both(later, pos == source))
        def _():
            for p in targets:
                w_copy(p).start()

    def send_extra(indices):
        @pl.when(gives_extra)
        def _():
            for index in indices:
                extra_copy(index).start()

    def pass_w(target, qs):
        @pl.when(both(later, pos == target))
        def _():
            for q in qs:
                w_arrival(q).wait_recv()
                y_copy(q).start()

    for tap in range(TAPS):
        fine_load(0, tap).wait()
    send_extra(range(PIECES // 2))
    send_w(0, (1, 2))
    send_w(1, (3,))
    send_w(2, (3,))

    z_index = lax.broadcasted_iota(jnp.int32, (size_x * size_y, size_z, width), 1)

    def mix(state, weights):
        squashed = jnp.tanh(state).reshape(size_x * size_y, size_z, width)
        below = jnp.where(z_index == 0, 0.0, pltpu.roll(squashed, 1, 1))
        above = jnp.where(z_index == size_z - 1, 0.0, pltpu.roll(squashed, size_z - 1, 1))
        span = size_y * size_z
        edge = jnp.zeros((size_x, size_z, width), jnp.float32)
        for tap_z, shifted in enumerate((below, squashed, above)):
            shifted = shifted.reshape(size_x, span, width)
            even = shifted.astype(jnp.bfloat16)
            odd = jnp.concatenate([edge, shifted, edge], 1).astype(jnp.bfloat16)
            for tap_y, block in enumerate((odd[:, :span], even, odd[:, 2 * size_z:])):
                column = (tap_y * TAPS + tap_z) * width
                patches[:, :, column:column + width] = block
        left = patches[...].reshape(size_x * span, rows)
        product = jnp.dot(left, weights[...], preferred_element_type=jnp.float32)
        product = product.reshape(size_x, size_y, size_z, TAPS * width)
        plane = jnp.zeros((1, size_y, size_z, width), jnp.float32)
        total = product[..., width:2 * width]
        total = total + jnp.concatenate([plane, product[:-1, :, :, :width]], 0)
        return total + jnp.concatenate([product[1:, :, :, 2 * width:], plane], 0)

    def fine_step(layer):
        state = cur[...]
        mixed = mix(state, fine_w.at[layer])
        return state, mixed, state + fine_size * (mixed + bias_ref[layer])

    pl.when(me > 0)(first_hop.wait_recv)
    inputs_load.wait()
    bias_load.wait()
    cur[...] = jnp.where(is_first, inputs_ref[...], first_head[...])

    for layer in range(1, depth):
        for tap in range(TAPS):
            fine_load(layer, tap).wait()

    def sweep_one(layer, carry):
        after = fine_step(layer)[2]
        cur[...] = after
        states_ref[layer, 0] = after
        return carry

    lax.fori_loop(0, depth, sweep_one, 0)
    corner_out[...] = cur[...]
    pl.when(has_next)(second_hop.start)
    send_extra(range(PIECES // 2, PIECES))
    send_w(1, (2,))
    pass_w(1, (0,))
    pass_w(2, (0,))
    pass_w(3, (1, 2))

    def seed_copy(p):
        return remote(seed_out, seed_in, seed_send.at[p], seed_recv, device(p))

    def gives_seed(p):
        exact = both(opening, pos == 1)
        if p == last:
            handed = both(opening, both(pos == 2, core == 1))
            return either(both(later, pos == 0), either(both(exact, core == 0), handed))
        return exact

    takes_seed = either(is_last_pos, both(opening, pos == last - 1))

    def g_copy(p):
        return remote(defects.at[pos], defects.at[pos], g_send.at[p], g_recv.at[pos], device(p))

    def g_arrival(q):
        return remote(defects.at[q], defects.at[q], g_send.at[0], g_recv.at[q], device(q))

    def gives_g(p):
        if p == last:
            return both(pos < p, either(later, both(pos == last - 1, core == 0)))
        ahead = both(pos < p, later)
        return either(ahead, both(opening, both(is_last_pos, core == 1))) if p == last - 1 else ahead

    @pl.when(me > 0)
    def _():
        second_hop.wait_recv()
        send_w(0, (3,))
        head[...] = next_head[...]
        cur[...] = next_head[...]

        def sweep_two(layer, carry):
            _, mixed, after = fine_step(layer)

            @pl.when(layer == 0)
            def _():
                head_mix[...] = mixed

            cur[...] = after
            states_ref[layer, 0] = after
            return carry

        lax.fori_loop(0, depth, sweep_two, 0)
        seed_out[...] = cur[...]

        @pl.when(opening)
        def _():
            pl.when(both(gives_seed(last), pos == 1))(seed_copy(last).start)
            pl.when(gives_seed(last - 1))(seed_copy(last - 1).start)

        defects[pos] = cur[...] - head[...] - coarse_size * head_mix[...]
        for p in (last, last - 1, 1):
            pl.when(gives_g(p))(g_copy(p).start)
        pl.when(both(later, gives_seed(last)))(seed_copy(last).start)

    pass_w(2, (1,))
    pass_w(3, (0,))

    for q in range(last):
        @pl.when(both(later, pos > q))
        def _(q=q):
            y_copy(q).wait_recv()
            sib_copy(q).start()

    for q in range(last):
        @pl.when(both(later, pos > q))
        def _(q=q):
            sib_copy(q).wait_recv()
            g_arrival(q).wait_recv()

    def own_step():
        state = cur[...]
        mixed = mix(state, fine_w.at[0])
        head[...] = state
        head_mix[...] = mixed
        return state + coarse_size * mixed + defects[pos]

    def chain(low, high):
        def step(turn, carry):
            state = cur[...]
            cur[...] = state + coarse_size * mix(state, lead_w.at[turn]) + defects[turn]
            return carry

        lax.fori_loop(low, high, step, 0)

    def extra_step(q):
        state = cur[...]
        for index in range(PIECES):
            extra_copy(index).wait_recv()
        mixed = mix(state, lead_w.at[extra])
        g_arrival(q).wait_recv()
        cur[...] = state + coarse_size * mixed + defects[q]

    def top_copy(p):
        return remote(top_out, top_in, top_send.at[p], top_recv, device(p, 1))

    def send_top():
        for p in range(last, -1, -1):
            top_copy(p).start()

    start_copy = remote(c_point, start_in, start_send, start_recv, device(last, 1))

    @pl.when(both(opening, is_upper))
    def _():
        seed_copy(0).wait_recv()
        cur[...] = seed_in[...]

        @pl.when(both(is_last_pos, finishes))
        def _():
            extra_step(last - 1)

        after = own_step()
        states_ref[last, 0] = after
        cur[...] = after

        @pl.when(both(pos == last - 1, finishes))
        def _():
            seed_out[...] = after
            seed_copy(last).start()
            extra_step(last)

        @pl.when(both(finishes, has_group_after))
        def _():
            top_out[...] = cur[...]
            send_top()

    def relax_again():
        seed_copy(0).wait_recv()
        cur[...] = seed_in[...]
        chain(1, last)
        c_point[...] = own_step()

    ends_later = both(is_last_pos, later)

    @pl.when(both(ends_later, has_group_after))
    def _():
        relax_again()
        start_copy.start()

    has_start = both(is_last_pos, group > 1)

    @pl.when(has_start)
    def _():
        start_copy.wait_recv()
        cur[...] = start_in[...]
        chain(0, last)
        corner = own_step()
        residual_ref[0, 0] = corner
        start = start_in[...]
        top_out[...] = corner - start - top_size * mix(start, fine_w.at[0])

    @pl.when(later)
    def _():
        top_copy(0).wait_recv()

    @pl.when(has_start)
    def _():
        solved = top_in[...]
        top_out[...] = solved + top_size * mix(solved, fine_w.at[0]) + top_out[...]
        pl.when(has_group_after)(send_top)

    @pl.when(later)
    def _():
        cur[...] = top_in[...]
        chain(0, pos)
        after = own_step()
        states_ref[last, 0] = jnp.where(has_start, top_out[...], after)

        @pl.when(jnp.logical_not(has_start))
        def _():
            residual_ref[0, 0] = after

        @pl.when(both(both(is_last_pos, group == 1), has_group_after))
        def _():
            top_out[...] = after
            send_top()

    @pl.when(opening)
    def _():
        residual_ref[0, 0] = states_ref[last, 0]

    @pl.when(me > 1)
    def _():
        cur[...] = head[...] + fine_size * (head_mix[...] + bias_ref[0])
        states_ref[0, 0] = cur[...]

        def last_sweep(layer, carry):
            after = fine_step(layer)[2]
            cur[...] = after
            states_ref[layer, 0] = after
            return carry

        lax.fori_loop(1, depth - 1, last_sweep, 0)

    @pl.when(both(ends_later, jnp.logical_not(has_group_after)))
    def _():
        relax_again()

    corner = residual_ref[0, 0]
    residual_ref[0, 0] = corner - jnp.where(ends_later, c_point[...], corner)

    pl.when(has_next)(first_hop.wait_send)
    pl.when(has_next)(second_hop.wait_send)
    for p in range(1, COARSEN):
        pl.when(both(later, pos < p))(w_copy(p).wait_send)
        pl.when(gives_g(p))(g_copy(p).wait_send)
        if p > 1:
            pl.when(gives_seed(p))(seed_copy(p).wait_send)
    for q in range(last):
        pl.when(both(later, pos > q))(y_copy(q).wait_send)
        pl.when(both(later, pos > q))(sib_copy(q).wait_send)

    @pl.when(gives_extra)
    def _():
        for index in range(PIECES):
            extra_copy(index).wait_send()

    @pl.when(both(has_group_after, either(finishes, ends_later)))
    def _():
        for p in range(COARSEN):
            top_copy(p).wait_send()

    pl.when(both(ends_later, has_group_after))(start_copy.wait_send)


def shards(inputs, guess_states, kernels, biases):
    sections = lax.axis_size("layer")
    depth = guess_states.shape[0]
    state = inputs.shape[1:]
    width = state[-1]
    rows = TAPS * TAPS * width
    vmem = pl.BlockSpec(memory_space=pltpu.VMEM)
    hbm = pl.BlockSpec(memory_space=pltpu.HBM)
    kernel_rows = kernels.reshape(depth, TAPS, rows, width)
    bias_rows = biases.reshape(depth, 1, 1, width)
    f32_state = pltpu.VMEM(state, jnp.float32)
    dma = pltpu.SemaphoreType.DMA
    operands = [pltpu.with_memory_space_constraint(operand, pltpu.HBM)
                for operand in (inputs.reshape(state), guess_states, kernel_rows, bias_rows)]

    def body(*refs):
        cycle_kernel(sections, *refs)

    return tuple(pl.pallas_call(
        body,
        name="mgrit_cycle",
        out_shape=(
            pltpu.VMEM(guess_states.shape, jnp.float32),
            pltpu.VMEM((1,) + guess_states.shape[1:], jnp.float32),
        ),
        in_specs=[hbm, hbm, hbm, hbm],
        out_specs=(vmem, vmem),
        scratch_shapes=[
            f32_state, pltpu.VMEM(bias_rows.shape, jnp.float32),
            pltpu.VMEM((depth, rows, TAPS * width), jnp.bfloat16),
            pltpu.VMEM((COARSEN - 1, rows, TAPS * width), jnp.bfloat16),
            pltpu.VMEM((state[0], state[1] * state[2], rows), jnp.bfloat16),
            f32_state, f32_state, f32_state, f32_state, f32_state, f32_state,
            f32_state, f32_state, f32_state, f32_state, f32_state, f32_state,
            pltpu.VMEM((COARSEN,) + state, jnp.float32),
            dma((depth, TAPS)), dma((2,)), dma((2,)), dma((2,)),
            dma((COARSEN,)), dma((COARSEN - 1,)), dma((COARSEN - 1,)), dma((COARSEN - 1,)),
            dma((COARSEN - 1,)), dma((COARSEN - 1,)), dma((PIECES,)), dma((PIECES,)),
            dma((COARSEN,)), dma((COARSEN,)), dma((COARSEN,)), dma, dma, dma, dma((COARSEN,)), dma,
        ],
        compiler_params=pltpu.CompilerParams(
            collective_id=0, has_side_effects=True, vmem_limit_bytes=24 * 1024 * 1024),
    )(*operands))


def solution(mesh):
    return jax.shard_map(
        shards,
        mesh=mesh,
        in_specs=(
            P("batch", None, None, None, None),
            P("layer", "batch", None, None, None, None),
            P("layer", None, None, None, None, None),
            P("layer", None),
        ),
        out_specs=(
            P("layer", "batch", None, None, None, None),
            P("layer", "batch", None, None, None, None),
        ),
        check_vma=False,
    )
```

```python
import jax
import jax.numpy as jnp
from jax import lax
from jax.experimental import pallas as pl
from jax.experimental.pallas import tpu as pltpu
from jax.sharding import PartitionSpec as P

COARSEN = 4
TAPS = 3
PIECES = 4
MESH = pl.DeviceIdType.MESH


def cycle_kernel(sections, inputs_hbm, guess_ref, kern_ref, bias_hbm, states_ref, residual_ref,
                 inputs_ref, bias_ref, fine_w, lead_w, patches, cur, head, head_mix,
                 first_head, next_head, corner_out, seed_out, seed_in, c_point,
                 start_in, top_in, top_out, defects,
                 load_sem, small_sem, hop_send, hop_recv, w_send, w_recv, y_send, y_recv, sib_send, sib_recv,
                 extra_send, extra_recv, cross_send, cross_recv, gate,
                 g_send, g_recv, seed_send, seed_recv, origin_send, start_send, start_recv, top_send, top_recv, relay_send, turn_send):
    depth = guess_ref.shape[0]
    size_x, size_y, size_z, width = inputs_ref.shape
    groups = sections // COARSEN
    fine_size = 2.0 / (depth * sections)
    coarse_size = depth * fine_size
    top_size = COARSEN * coarse_size
    rows = TAPS * TAPS * width
    piece_rows = rows // PIECES
    last = COARSEN - 1
    extra = COARSEN - 2
    span = COARSEN // 2
    me = lax.axis_index("layer")
    part = lax.axis_index("batch")
    pos = lax.rem(me, COARSEN)
    group = me // COARSEN
    core = lax.rem(part, 2)
    row = lax.rem(part // 2, 2)
    sibling = part + 1 - 2 * core
    across = part + 2 - 4 * row
    both = jnp.logical_and
    either = jnp.logical_or
    is_first = me == 0
    has_next = me < sections - 1
    later = group > 0
    opening = group == 0
    has_group_after = group < groups - 1
    is_last_pos = pos == last
    is_upper = pos >= last - 1

    def device(p, ahead=0):
        return ((group + ahead) * COARSEN + p, part)

    barrier = pltpu.get_barrier_semaphore()

    def greet(target):
        pl.semaphore_signal(barrier, inc=1, device_id=target, device_id_type=MESH)

    for rel in range(1, COARSEN):
        greet(device(lax.rem(pos + rel, COARSEN)))
    greet((me, sibling))
    greet((me, across))
    greets_ahead = both(is_upper, has_group_after)

    @pl.when(greets_ahead)
    def _():
        for p in range(COARSEN):
            greet(device(p, 1))

    @pl.when(later)
    def _():
        for p in (last - 1, last):
            greet(device(p, -1))

    def fine_load(layer, tap):
        return pltpu.make_async_copy(
            kern_ref.at[layer, tap],
            fine_w.at[layer, :, pl.ds(tap * width, width)],
            load_sem.at[layer, tap],
        )

    inputs_load = pltpu.make_async_copy(inputs_hbm, inputs_ref, small_sem.at[0])
    bias_load = pltpu.make_async_copy(bias_hbm, bias_ref, small_sem.at[1])
    inputs_load.start()
    bias_load.start()
    for layer in range(depth):
        for tap in range(TAPS):
            fine_load(layer, tap).start()

    greetings = COARSEN + 1 + jnp.where(greets_ahead, COARSEN, 0) + jnp.where(later, 2, 0)
    pl.semaphore_wait(barrier, greetings)

    def remote(source, target, send_sem, recv_sem, where):
        return pltpu.make_async_remote_copy(
            src_ref=source, dst_ref=target, send_sem=send_sem, recv_sem=recv_sem,
            device_id=where, device_id_type=MESH)

    def hop(index, source, target):
        return remote(source, target, hop_send.at[index], hop_recv.at[index], (me + 1, part))

    first_hop = hop(0, guess_ref.at[depth - 1, 0], first_head)
    second_hop = hop(1, corner_out, next_head)
    staggers = both(has_next, me < 2)
    leads = both(staggers, core == jnp.where(me == 1, 1, 0))
    trails = both(staggers, jnp.logical_not(leads))
    pl.when(both(has_next, jnp.logical_not(trails)))(first_hop.start)

    def open_gate(index):
        pl.semaphore_signal(gate.at[index], inc=1, device_id=(me, sibling), device_id_type=MESH)


    slot = jnp.minimum(pos, last - 1)
    quarter = pl.ds(pl.multiple_of((core * 2 + row) * piece_rows, 16), piece_rows)
    half = pl.ds(pl.multiple_of(core * 2 * piece_rows, 16), 2 * piece_rows)

    def w_copy(p):
        return remote(fine_w.at[0, quarter], lead_w.at[slot, quarter], w_send.at[p], w_recv.at[slot], device(p))

    def w_arrival(q):
        return remote(lead_w.at[q, quarter], lead_w.at[q, quarter], w_send.at[0], w_recv.at[q], device(q))

    w_turn = remote(lead_w.at[1, quarter], lead_w.at[1, quarter], turn_send.at[0], w_recv.at[1], device(last - 1))

    def y_copy(q):
        return remote(lead_w.at[q, quarter], lead_w.at[q, quarter], y_send.at[q], y_recv.at[q], (me, across))

    def sib_copy(q):
        return remote(lead_w.at[q, half], lead_w.at[q, half], sib_send.at[q], sib_recv.at[q], (me, sibling))

    def extra_copy(index):
        piece = pl.ds(pl.multiple_of((row * 2 + index) * piece_rows, 16), piece_rows)
        return remote(fine_w.at[0, piece], lead_w.at[extra, piece], extra_send.at[index], extra_recv.at[index],
                      device(2 * last - 1 - pos))

    def cross_copy(index):
        piece = pl.ds(pl.multiple_of((row * 2 + index) * piece_rows, 16), piece_rows)
        return remote(lead_w.at[extra, piece], lead_w.at[extra, piece], cross_send.at[index], cross_recv.at[index],
                      (me, across))

    gives_extra = both(opening, either(both(pos == last - 1, core == 0), both(pos == last, core == 1)))
    finishes = both(opening, either(both(pos == last, core == 0), both(pos == last - 1, core == 1)))

    def send_w(source, targets):
        @pl.when(both(later, pos == source))
        def _():
            for p in targets:
                w_copy(p).start()

    halves = range(PIECES // 2)

    def send_extra(source):
        @pl.when(both(gives_extra, pos == source))
        def _():
            for index in halves:
                extra_copy(index).start()

    def pass_extra(target):
        @pl.when(both(finishes, pos == target))
        def _():
            for index in halves:
                extra_copy(index).wait_recv()
                cross_copy(index).start()

    def first_wave():
        send_w(0, (1, 2))
        send_w(1, (3,))
        send_w(2, (3,))

    def pass_w(target, qs):
        @pl.when(both(later, pos == target))
        def _():
            for q in qs:
                w_arrival(q).wait_recv()
                y_copy(q).start()
                if target == last and q == 1:
                    w_turn.start()

    for tap in range(TAPS):
        fine_load(0, tap).wait()
    send_extra(last - 1)
    inputs_load.wait()
    bias_load.wait()
    for layer in range(1, depth):
        for tap in range(TAPS):
            fine_load(layer, tap).wait()
    send_extra(last)

    def let_pass():
        first_hop.wait_send()
        open_gate(0)

    def follow():
        pl.semaphore_wait(gate.at[0], 1)
        first_hop.start()

    first_wave()
    pl.when(both(leads, me > 0))(let_pass)
    pl.when(both(trails, me > 0))(follow)

    z_index = lax.broadcasted_iota(jnp.int32, (size_x * size_y, size_z, width), 1)

    def mix(state, weights):
        squashed = jnp.tanh(state).reshape(size_x * size_y, size_z, width)
        below = jnp.where(z_index == 0, 0.0, pltpu.roll(squashed, 1, 1))
        above = jnp.where(z_index == size_z - 1, 0.0, pltpu.roll(squashed, size_z - 1, 1))
        span = size_y * size_z
        edge = jnp.zeros((size_x, size_z, width), jnp.float32)
        for tap_z, shifted in enumerate((below, squashed, above)):
            shifted = shifted.reshape(size_x, span, width)
            even = shifted.astype(jnp.bfloat16)
            odd = jnp.concatenate([edge, shifted, edge], 1).astype(jnp.bfloat16)
            for tap_y, block in enumerate((odd[:, :span], even, odd[:, 2 * size_z:])):
                column = (tap_y * TAPS + tap_z) * width
                patches[:, :, column:column + width] = block
        left = patches[...].reshape(size_x * span, rows)
        product = jnp.dot(left, weights[...], preferred_element_type=jnp.float32)
        product = product.reshape(size_x, size_y, size_z, TAPS * width)
        plane = jnp.zeros((1, size_y, size_z, width), jnp.float32)
        total = product[..., width:2 * width]
        total = total + jnp.concatenate([plane, product[:-1, :, :, :width]], 0)
        return total + jnp.concatenate([product[1:, :, :, 2 * width:], plane], 0)

    def fine_step(layer):
        state = cur[...]
        mixed = mix(state, fine_w.at[layer])
        return state, mixed, state + fine_size * (mixed + bias_ref[layer])

    pl.when(me > 0)(first_hop.wait_recv)
    cur[...] = jnp.where(is_first, inputs_ref[...], first_head[...])

    def sweep_one(layer, carry):
        after = fine_step(layer)[2]
        cur[...] = after
        states_ref[layer, 0] = after
        pl.when(both(both(leads, is_first), layer == depth - 2))(let_pass)
        pl.when(both(both(trails, is_first), layer == depth - 2))(follow)
        return carry

    lax.fori_loop(0, depth, sweep_one, 0)
    corner_out[...] = cur[...]
    pl.when(has_next)(second_hop.start)
    origin_copy = remote(corner_out, seed_in, origin_send, seed_recv, device(last, 1))
    sends_origin = both(is_last_pos, has_group_after)
    pl.when(sends_origin)(origin_copy.start)
    pass_extra(last)
    pass_w(1, (0,))
    pass_w(2, (0,))
    pass_w(3, (1, 2))

    def seed_copy(p):
        return remote(seed_out, seed_in, seed_send.at[p], seed_recv, device(p))

    def gives_seed(p):
        exact = both(opening, pos == 1)
        if p == last:
            handed = both(opening, both(pos == 2, core == 1))
            return either(both(exact, core == 0), handed)
        return exact

    takes_seed = either(is_last_pos, both(opening, pos == last - 1))

    def g_copy(p):
        return remote(defects.at[pos], defects.at[pos], g_send.at[p], g_recv.at[pos], device(p))

    def g_arrival(q):
        return remote(defects.at[q], defects.at[q], g_send.at[0], g_recv.at[q], device(q))

    def gives_g(p):
        if p == last:
            return both(pos < p, either(later, both(pos == last - 1, core == 0)))
        ahead = both(pos < (1 if p == last - 1 else p), later)
        return either(ahead, both(opening, both(is_last_pos, core == 1))) if p == last - 1 else ahead

    @pl.when(me > 0)
    def _():
        second_hop.wait_recv()
        send_w(0, (3,))
        pass_extra(last - 1)
        head[...] = next_head[...]
        cur[...] = next_head[...]

        def sweep_two(layer, carry):
            _, mixed, after = fine_step(layer)

            @pl.when(layer == 0)
            def _():
                head_mix[...] = mixed

            cur[...] = after
            states_ref[layer, 0] = after
            return carry

        lax.fori_loop(0, depth, sweep_two, 0)

        @pl.when(opening)
        def _():
            seed_out[...] = cur[...]
            pl.when(both(gives_seed(last), pos == 1))(seed_copy(last).start)
            pl.when(both(gives_seed(last - 1), core == 1))(seed_copy(last - 1).start)

        defects[pos] = cur[...] - head[...] - coarse_size * head_mix[...]
        for p in (last, last - 1, 1):
            pl.when(gives_g(p))(g_copy(p).start)

    g_turn = remote(defects.at[1], defects.at[1], turn_send.at[1], g_recv.at[1], device(last - 1))

    pass_w(2, (1,))
    pass_w(3, (0,))

    @pl.when(both(later, is_last_pos))
    def _():
        g_arrival(1).wait_recv()
        g_turn.start()

    for q in range(last):
        @pl.when(both(later, pos > q))
        def _(q=q):
            y_copy(q).wait_recv()
            sib_copy(q).start()

    ends_later = both(is_last_pos, later)
    waits_first = both(ends_later, has_group_after)

    for q in range(last):
        @pl.when(both(waits_first, pos > q))
        def _(q=q):
            sib_copy(q).wait_recv()
            if q != 1:
                g_arrival(q).wait_recv()

    def own_step():
        state = cur[...]
        mixed = mix(state, fine_w.at[0])
        head[...] = state
        head_mix[...] = mixed
        return state + coarse_size * mixed + defects[pos]

    def chain(low, high, arriving=False):
        def step(turn, carry):
            state = cur[...]
            if arriving:
                pl.when(jnp.logical_not(waits_first))(sib_copy(turn).wait_recv)
            mixed = mix(state, lead_w.at[turn])
            if arriving:
                waits_g = jnp.logical_not(either(waits_first, both(is_last_pos, turn == 1)))
                pl.when(waits_g)(g_arrival(turn).wait_recv)
            cur[...] = state + coarse_size * mixed + defects[turn]
            return carry

        lax.fori_loop(low, high, step, 0)

    def extra_step(q):
        state = cur[...]
        for index in halves:
            cross_copy(index).wait_recv()
        mixed = mix(state, lead_w.at[extra])
        g_arrival(q).wait_recv()
        cur[...] = state + coarse_size * mixed + defects[q]

    half_planes = size_x // 2
    direct = [(p, h) for p in range(last, -1, -1) for h in range(2) if p >= span or h == 1]

    def top_copy(p, h):
        planes = pl.ds(h * half_planes, half_planes)
        return remote(top_out.at[planes], top_in.at[planes], top_send.at[p, h], top_recv.at[h], device(p, 1))

    def top_relay():
        planes = pl.ds(0, half_planes)
        return remote(top_in.at[planes], top_in.at[planes], relay_send, top_recv.at[0], device(pos - span))

    relays_top = both(later, pos >= span)

    def send_top():
        for p, h in direct:
            top_copy(p, h).start()

    start_copy = remote(c_point, start_in, start_send, start_recv, device(last, 1))

    @pl.when(both(opening, is_upper))
    def _():
        seed_copy(0).wait_recv()
        cur[...] = seed_in[...]

        @pl.when(both(is_last_pos, finishes))
        def _():
            extra_step(last - 1)

        after = own_step()
        states_ref[last, 0] = after
        cur[...] = after

        @pl.when(both(pos == last - 1, finishes))
        def _():
            seed_out[...] = after
            seed_copy(last).start()
            extra_step(last)

        @pl.when(both(finishes, has_group_after))
        def _():
            top_out[...] = cur[...]
            send_top()

    def relax_again():
        seed_copy(0).wait_recv()
        cur[...] = seed_in[...]
        chain(0, last)
        c_point[...] = own_step()

    @pl.when(waits_first)
    def _():
        relax_again()
        start_copy.start()

    has_start = both(is_last_pos, group > 1)

    @pl.when(has_start)
    def _():
        start_copy.wait_recv()
        cur[...] = start_in[...]
        chain(0, last)
        corner = own_step()
        residual_ref[0, 0] = corner
        start = start_in[...]
        top_out[...] = corner - start - top_size * mix(start, fine_w.at[0])

    @pl.when(later)
    def _():
        top_copy(0, 0).wait_recv()
        pl.when(relays_top)(lambda: top_relay().start())
        top_copy(0, 1).wait_recv()

    @pl.when(has_start)
    def _():
        solved = top_in[...]
        top_out[...] = solved + top_size * mix(solved, fine_w.at[0]) + top_out[...]
        pl.when(has_group_after)(send_top)

    @pl.when(later)
    def _():
        cur[...] = top_in[...]
        chain(0, pos, arriving=True)
        after = own_step()
        states_ref[last, 0] = jnp.where(has_start, top_out[...], after)

        @pl.when(jnp.logical_not(has_start))
        def _():
            residual_ref[0, 0] = after

        @pl.when(both(both(is_last_pos, group == 1), has_group_after))
        def _():
            top_out[...] = after
            send_top()

    @pl.when(opening)
    def _():
        residual_ref[0, 0] = states_ref[last, 0]

    @pl.when(me > 1)
    def _():
        cur[...] = head[...] + fine_size * (head_mix[...] + bias_ref[0])
        states_ref[0, 0] = cur[...]

        def last_sweep(layer, carry):
            after = fine_step(layer)[2]
            cur[...] = after
            states_ref[layer, 0] = after
            return carry

        lax.fori_loop(1, depth - 1, last_sweep, 0)

    @pl.when(both(ends_later, jnp.logical_not(has_group_after)))
    def _():
        relax_again()

    corner = residual_ref[0, 0]
    residual_ref[0, 0] = corner - jnp.where(ends_later, c_point[...], corner)

    hands_on = both(both(opening, pos == 1), core == 0)

    @pl.when(both(both(opening, pos == 1), core == 1))
    def _():
        seed_copy(last - 1).wait_send()
        open_gate(1)

    @pl.when(hands_on)
    def _():
        pl.semaphore_wait(gate.at[1], 1)
        seed_copy(last - 1).start()

    pl.when(both(has_next, jnp.logical_not(leads)))(first_hop.wait_send)
    pl.when(has_next)(second_hop.wait_send)
    for p in range(1, COARSEN):
        pl.when(both(later, pos < (1 if p == last - 1 else p)))(w_copy(p).wait_send)
        pl.when(gives_g(p))(g_copy(p).wait_send)
    pl.when(gives_seed(last))(seed_copy(last).wait_send)
    pl.when(sends_origin)(origin_copy.wait_send)
    pl.when(hands_on)(seed_copy(last - 1).wait_send)
    for q in range(last):
        pl.when(both(later, pos > q))(y_copy(q).wait_send)
        pl.when(both(later, pos > q))(sib_copy(q).wait_send)

    @pl.when(ends_later)
    def _():
        w_turn.wait_send()
        g_turn.wait_send()

    @pl.when(gives_extra)
    def _():
        for index in halves:
            extra_copy(index).wait_send()

    @pl.when(finishes)
    def _():
        for index in halves:
            cross_copy(index).wait_send()

    @pl.when(both(has_group_after, either(finishes, ends_later)))
    def _():
        for p, h in direct:
            top_copy(p, h).wait_send()

    pl.when(relays_top)(lambda: top_relay().wait_send())

    pl.when(both(ends_later, has_group_after))(start_copy.wait_send)


def shards(inputs, guess_states, kernels, biases):
    sections = lax.axis_size("layer")
    depth = guess_states.shape[0]
    state = inputs.shape[1:]
    width = state[-1]
    rows = TAPS * TAPS * width
    vmem = pl.BlockSpec(memory_space=pltpu.VMEM)
    hbm = pl.BlockSpec(memory_space=pltpu.HBM)
    kernel_rows = kernels.reshape(depth, TAPS, rows, width)
    bias_rows = biases.reshape(depth, 1, 1, width)
    f32_state = pltpu.VMEM(state, jnp.float32)
    dma = pltpu.SemaphoreType.DMA
    operands = [pltpu.with_memory_space_constraint(operand, pltpu.HBM)
                for operand in (inputs.reshape(state), guess_states, kernel_rows, bias_rows)]

    def body(*refs):
        cycle_kernel(sections, *refs)

    return tuple(pl.pallas_call(
        body,
        name="mgrit_cycle",
        out_shape=(
            pltpu.VMEM(guess_states.shape, jnp.float32),
            pltpu.VMEM((1,) + guess_states.shape[1:], jnp.float32),
        ),
        in_specs=[hbm, hbm, hbm, hbm],
        out_specs=(vmem, vmem),
        scratch_shapes=[
            f32_state, pltpu.VMEM(bias_rows.shape, jnp.float32),
            pltpu.VMEM((depth, rows, TAPS * width), jnp.bfloat16),
            pltpu.VMEM((COARSEN - 1, rows, TAPS * width), jnp.bfloat16),
            pltpu.VMEM((state[0], state[1] * state[2], rows), jnp.bfloat16),
            f32_state, f32_state, f32_state, f32_state, f32_state, f32_state,
            f32_state, f32_state, f32_state, f32_state, f32_state, f32_state,
            pltpu.VMEM((COARSEN,) + state, jnp.float32),
            dma((depth, TAPS)), dma((2,)), dma((2,)), dma((2,)),
            dma((COARSEN,)), dma((COARSEN - 1,)), dma((COARSEN - 1,)), dma((COARSEN - 1,)),
            dma((COARSEN - 1,)), dma((COARSEN - 1,)), dma((PIECES // 2,)), dma((PIECES // 2,)),
            dma((PIECES // 2,)), dma((PIECES // 2,)), pltpu.SemaphoreType.REGULAR((2,)),
            dma((COARSEN,)), dma((COARSEN,)), dma((COARSEN,)), dma, dma, dma, dma,
            dma((COARSEN, 2)), dma((2,)), dma, dma((2,)),
        ],
        compiler_params=pltpu.CompilerParams(
            collective_id=0, has_side_effects=True, vmem_limit_bytes=24 * 1024 * 1024),
    )(*operands))


def solution(mesh):
    return jax.shard_map(
        shards,
        mesh=mesh,
        in_specs=(
            P("batch", None, None, None, None),
            P("layer", "batch", None, None, None, None),
            P("layer", None, None, None, None, None),
            P("layer", None),
        ),
        out_specs=(
            P("layer", "batch", None, None, None, None),
            P("layer", "batch", None, None, None, None),
        ),
        check_vma=False,
    )
```

```python
import jax
import jax.numpy as jnp
from jax import lax
from jax.experimental import pallas as pl
from jax.experimental.pallas import tpu as pltpu
from jax.sharding import PartitionSpec as P

COARSEN = 4
TAPS = 3
PIECES = 4
MESH = pl.DeviceIdType.MESH


def cycle_kernel(sections, inputs_hbm, guess_ref, kern_ref, bias_hbm, states_ref, residual_ref,
                 inputs_ref, bias_ref, fine_w, lead_w, patches, cur, head, head_mix,
                 first_head, next_head, corner_out, seed_out, seed_in, c_point,
                 start_in, top_in, top_out, defects,
                 load_sem, small_sem, hop_send, hop_recv, w_send, w_recv, y_send, y_recv, sib_send, sib_recv,
                 extra_send, extra_recv, cross_send, cross_recv, gate,
                 g_send, g_recv, seed_send, seed_recv, origin_send, start_send, start_recv, top_send, top_recv, relay_send, turn_send, back_send, ahead_send):
    depth = guess_ref.shape[0]
    size_x, size_y, size_z, width = inputs_ref.shape
    groups = sections // COARSEN
    fine_size = 2.0 / (depth * sections)
    coarse_size = depth * fine_size
    top_size = COARSEN * coarse_size
    rows = TAPS * TAPS * width
    piece_rows = rows // PIECES
    last = COARSEN - 1
    extra = COARSEN - 2
    span = COARSEN // 2
    me = lax.axis_index("layer")
    part = lax.axis_index("batch")
    pos = lax.rem(me, COARSEN)
    group = me // COARSEN
    core = lax.rem(part, 2)
    row = lax.rem(part // 2, 2)
    sibling = part + 1 - 2 * core
    across = part + 2 - 4 * row
    both = jnp.logical_and
    either = jnp.logical_or
    is_first = me == 0
    has_next = me < sections - 1
    later = group > 0
    opening = group == 0
    has_group_after = group < groups - 1
    is_last_pos = pos == last
    is_upper = pos >= last - 1

    def device(p, ahead=0):
        return ((group + ahead) * COARSEN + p, part)

    barrier = pltpu.get_barrier_semaphore()

    def greet(target):
        pl.semaphore_signal(barrier, inc=1, device_id=target, device_id_type=MESH)

    for rel in range(1, COARSEN):
        greet(device(lax.rem(pos + rel, COARSEN)))
    greet((me, sibling))
    greet((me, across))
    greets_ahead = both(is_upper, has_group_after)

    @pl.when(greets_ahead)
    def _():
        for p in range(COARSEN):
            greet(device(p, 1))

    @pl.when(later)
    def _():
        for p in (last - 1, last):
            greet(device(p, -1))

    def fine_load(layer, tap):
        return pltpu.make_async_copy(
            kern_ref.at[layer, tap],
            fine_w.at[layer, :, pl.ds(tap * width, width)],
            load_sem.at[layer, tap],
        )

    inputs_load = pltpu.make_async_copy(inputs_hbm, inputs_ref, small_sem.at[0])
    bias_load = pltpu.make_async_copy(bias_hbm, bias_ref, small_sem.at[1])
    inputs_load.start()
    bias_load.start()
    for layer in range(depth):
        for tap in range(TAPS):
            fine_load(layer, tap).start()

    greetings = COARSEN + 1 + jnp.where(greets_ahead, COARSEN, 0) + jnp.where(later, 2, 0)
    pl.semaphore_wait(barrier, greetings)

    def remote(source, target, send_sem, recv_sem, where):
        return pltpu.make_async_remote_copy(
            src_ref=source, dst_ref=target, send_sem=send_sem, recv_sem=recv_sem,
            device_id=where, device_id_type=MESH)

    def hop(index, source, target):
        return remote(source, target, hop_send.at[index], hop_recv.at[index], (me + 1, part))

    first_hop = hop(0, guess_ref.at[depth - 1, 0], first_head)
    second_hop = hop(1, corner_out, next_head)
    staggers = both(has_next, me < 2)
    leads = both(staggers, core == jnp.where(me == 1, 1, 0))
    trails = both(staggers, jnp.logical_not(leads))
    waits_loads = both(core == 1, me > 1)
    pl.when(both(has_next, jnp.logical_not(either(trails, waits_loads))))(first_hop.start)

    def open_gate(index):
        pl.semaphore_signal(gate.at[index], inc=1, device_id=(me, sibling), device_id_type=MESH)


    slot = jnp.minimum(pos, last - 1)
    quarter = pl.ds(pl.multiple_of((core * 2 + row) * piece_rows, 16), piece_rows)
    half = pl.ds(pl.multiple_of(core * 2 * piece_rows, 16), 2 * piece_rows)

    def w_copy(p):
        return remote(fine_w.at[0, quarter], lead_w.at[slot, quarter], w_send.at[p], w_recv.at[slot], device(p))

    def w_arrival(q):
        return remote(lead_w.at[q, quarter], lead_w.at[q, quarter], w_send.at[0], w_recv.at[q], device(q))

    w_turn = remote(lead_w.at[1, quarter], lead_w.at[1, quarter], turn_send.at[0], w_recv.at[1], device(last - 1))

    def y_copy(q):
        return remote(lead_w.at[q, quarter], lead_w.at[q, quarter], y_send.at[q], y_recv.at[q], (me, across))

    def sib_copy(q):
        return remote(lead_w.at[q, half], lead_w.at[q, half], sib_send.at[q], sib_recv.at[q], (me, sibling))

    def extra_copy(index):
        piece = pl.ds(pl.multiple_of((row * 2 + index) * piece_rows, 16), piece_rows)
        return remote(fine_w.at[0, piece], lead_w.at[extra, piece], extra_send.at[index], extra_recv.at[index],
                      device(2 * last - 1 - pos))

    def cross_copy(index):
        piece = pl.ds(pl.multiple_of((row * 2 + index) * piece_rows, 16), piece_rows)
        return remote(lead_w.at[extra, piece], lead_w.at[extra, piece], cross_send.at[index], cross_recv.at[index],
                      (me, across))

    gives_extra = both(opening, either(both(pos == last - 1, core == 0), both(pos == last, core == 1)))
    finishes = both(opening, either(both(pos == last, core == 0), both(pos == last - 1, core == 1)))

    def send_w(source, targets):
        @pl.when(both(later, pos == source))
        def _():
            for p in targets:
                w_copy(p).start()

    halves = range(PIECES // 2)

    def send_extra(source):
        @pl.when(both(gives_extra, pos == source))
        def _():
            for index in halves:
                extra_copy(index).start()

    def pass_extra(target):
        @pl.when(both(finishes, pos == target))
        def _():
            for index in halves:
                extra_copy(index).wait_recv()
                cross_copy(index).start()

    w_ahead = remote(lead_w.at[0, quarter], lead_w.at[0, quarter], ahead_send, w_recv.at[0], device(last))
    back_slot = jnp.maximum(pos - 1, 0)
    w_back = remote(fine_w.at[0, quarter], lead_w.at[back_slot, quarter], back_send.at[0], w_recv.at[back_slot], device(0))

    def send_back(sources):
        for source in sources:
            pl.when(both(later, pos == source))(w_back.start)

    def holds(q):
        return both(later, either(pos > q, pos == 0))

    def first_wave():
        send_w(0, (2, 1))
        send_w(1, (3,))
        send_w(2, (3,))
        send_back((1, 2))

    def pass_w(target, qs):
        @pl.when(both(later, pos == target))
        def _():
            for q in qs:
                w_arrival(q).wait_recv()
                y_copy(q).start()
                if target == last and q == 1:
                    w_turn.start()

    for tap in range(TAPS):
        fine_load(0, tap).wait()
    send_extra(last - 1)
    inputs_load.wait()
    bias_load.wait()
    for layer in range(1, depth):
        for tap in range(TAPS):
            fine_load(layer, tap).wait()
    pl.when(both(has_next, waits_loads))(first_hop.start)
    send_extra(last)

    def let_pass():
        first_hop.wait_send()
        open_gate(0)

    def follow():
        pl.semaphore_wait(gate.at[0], 1)
        first_hop.start()

    first_wave()
    pl.when(both(leads, me > 0))(let_pass)
    pl.when(both(trails, me > 0))(follow)

    z_index = lax.broadcasted_iota(jnp.int32, (size_x * size_y, size_z, width), 1)

    def mix(state, weights):
        squashed = jnp.tanh(state).reshape(size_x * size_y, size_z, width)
        below = jnp.where(z_index == 0, 0.0, pltpu.roll(squashed, 1, 1))
        above = jnp.where(z_index == size_z - 1, 0.0, pltpu.roll(squashed, size_z - 1, 1))
        span = size_y * size_z
        edge = jnp.zeros((size_x, size_z, width), jnp.float32)
        for tap_z, shifted in enumerate((below, squashed, above)):
            shifted = shifted.reshape(size_x, span, width)
            even = shifted.astype(jnp.bfloat16)
            odd = jnp.concatenate([edge, shifted, edge], 1).astype(jnp.bfloat16)
            for tap_y, block in enumerate((odd[:, :span], even, odd[:, 2 * size_z:])):
                column = (tap_y * TAPS + tap_z) * width
                patches[:, :, column:column + width] = block
        left = patches[...].reshape(size_x * span, rows)
        product = jnp.dot(left, weights[...], preferred_element_type=jnp.float32)
        product = product.reshape(size_x, size_y, size_z, TAPS * width)
        plane = jnp.zeros((1, size_y, size_z, width), jnp.float32)
        total = product[..., width:2 * width]
        total = total + jnp.concatenate([plane, product[:-1, :, :, :width]], 0)
        return total + jnp.concatenate([product[1:, :, :, 2 * width:], plane], 0)

    def fine_step(layer):
        state = cur[...]
        mixed = mix(state, fine_w.at[layer])
        return state, mixed, state + fine_size * (mixed + bias_ref[layer])

    pl.when(me > 0)(first_hop.wait_recv)
    cur[...] = jnp.where(is_first, inputs_ref[...], first_head[...])

    def sweep_one(layer, carry):
        after = fine_step(layer)[2]
        cur[...] = after
        states_ref[layer, 0] = after
        pl.when(both(both(leads, is_first), layer == depth - 2))(let_pass)
        pl.when(both(both(trails, is_first), layer == depth - 2))(follow)
        return carry

    lax.fori_loop(0, depth, sweep_one, 0)
    corner_out[...] = cur[...]
    pl.when(has_next)(second_hop.start)
    pass_extra(last)
    pass_w(0, (1, 0))
    pass_w(1, (0,))
    pass_w(2, (0,))
    pass_w(3, (1, 2))

    def seed_copy(p):
        return remote(seed_out, seed_in, seed_send.at[p], seed_recv, device(p))

    def gives_seed(p):
        exact = both(opening, pos == 1)
        if p == last:
            handed = both(opening, both(pos == 2, core == 1))
            return either(both(exact, core == 0), handed)
        return exact

    takes_seed = either(is_last_pos, both(opening, pos == last - 1))

    def g_copy(p):
        return remote(defects.at[pos], defects.at[pos], g_send.at[p], g_recv.at[pos], device(p))

    def g_arrival(q):
        return remote(defects.at[q], defects.at[q], g_send.at[0], g_recv.at[q], device(q))

    def gives_g(p):
        if p == last:
            return both(pos < p, either(later, both(pos == last - 1, core == 0)))
        ahead = both(pos < (1 if p == last - 1 else p), later)
        return either(ahead, both(opening, both(is_last_pos, core == 1))) if p == last - 1 else ahead

    @pl.when(me > 0)
    def _():
        second_hop.wait_recv()
        pl.when(both(later, pos == 1))(w_ahead.start)
        send_back((3,))
        pass_extra(last - 1)
        head[...] = next_head[...]
        cur[...] = next_head[...]

        def sweep_two(layer, carry):
            _, mixed, after = fine_step(layer)

            @pl.when(layer == 0)
            def _():
                head_mix[...] = mixed

            cur[...] = after
            states_ref[layer, 0] = after
            return carry

        lax.fori_loop(0, depth, sweep_two, 0)

        @pl.when(opening)
        def _():
            seed_out[...] = cur[...]
            pl.when(both(gives_seed(last), pos == 1))(seed_copy(last).start)
            pl.when(both(gives_seed(last - 1), core == 1))(seed_copy(last - 1).start)

        defects[pos] = cur[...] - head[...] - coarse_size * head_mix[...]
        for p in (last, last - 1, 1):
            pl.when(gives_g(p))(g_copy(p).start)

    g_turn = remote(defects.at[1], defects.at[1], turn_send.at[1], g_recv.at[1], device(last - 1))

    g_back = remote(defects.at[pos], defects.at[pos], back_send.at[1], g_recv.at[pos], device(0))
    pl.when(both(later, both(pos > 0, pos < last)))(g_back.start)
    pass_w(2, (1,))
    pass_w(3, (0,))
    pass_w(0, (2,))


    for q in range(last):
        @pl.when(both(later, either(pos > q, both(pos == 0, q < last - 1))))
        def _(q=q):
            y_copy(q).wait_recv()
            sib_copy(q).start()

    ends_later = both(is_last_pos, later)
    def own_step():
        state = cur[...]
        mixed = mix(state, fine_w.at[0])
        head[...] = state
        head_mix[...] = mixed
        return state + coarse_size * mixed + defects[pos]

    def chain(low, high, arriving=False):
        def step(turn, carry):
            state = cur[...]
            if arriving:
                sib_copy(turn).wait_recv()
            mixed = mix(state, lead_w.at[turn])
            if arriving:
                pl.when(jnp.logical_not(both(is_last_pos, turn == 1)))(g_arrival(turn).wait_recv)
            cur[...] = state + coarse_size * mixed + defects[turn]
            return carry

        lax.fori_loop(low, high, step, 0)

    def extra_step(q):
        state = cur[...]
        for index in halves:
            cross_copy(index).wait_recv()
        mixed = mix(state, lead_w.at[extra])
        g_arrival(q).wait_recv()
        cur[...] = state + coarse_size * mixed + defects[q]

    half_planes = size_x // 2
    direct = [(0, 0), (0, 1), (2, 0), (2, 1), (1, 1)]
    targets = (last - core, last - span - core, core)

    def top_copy(p, h):
        planes = pl.ds(h * half_planes, half_planes)
        return remote(top_out.at[planes], top_in.at[planes], top_send.at[p, h], top_recv.at[h], device(targets[p], 1))

    def top_relay():
        planes = pl.ds(0, half_planes)
        return remote(top_in.at[planes], top_in.at[planes], relay_send.at[0], top_recv.at[0], device(pos - span))

    def top_side(h):
        planes = pl.ds(h * half_planes, half_planes)
        return remote(top_in.at[planes], top_in.at[planes], relay_send.at[h + 1], top_recv.at[h],
                      device(2 * last - 1 - pos))

    is_primary = both(later, pos == last - core)

    def send_top():
        for p, h in direct:
            top_copy(p, h).start()

    start_copy = remote(c_point, start_in, start_send, start_recv, device(last, 1))

    @pl.when(both(opening, is_upper))
    def _():
        seed_copy(0).wait_recv()
        cur[...] = seed_in[...]

        @pl.when(both(is_last_pos, finishes))
        def _():
            extra_step(last - 1)

        after = own_step()
        states_ref[last, 0] = after
        cur[...] = after

        @pl.when(both(pos == last - 1, finishes))
        def _():
            seed_out[...] = after
            seed_copy(last).start()
            extra_step(last)

        @pl.when(both(finishes, has_group_after))
        def _():
            top_out[...] = cur[...]
            send_top()

    relaxes = both(later, pos == 0)
    point_copy = remote(c_point, seed_in, origin_send, seed_recv, device(last))

    @pl.when(relaxes)
    def _():
        def step(turn, carry):
            state = cur[...]
            sib_copy(turn - 1).wait_recv()
            mixed = mix(state, lead_w.at[turn - 1])

            @pl.when(turn == last - 1)
            def _():
                y_copy(last - 1).wait_recv()
                sib_copy(last - 1).start()

            after = state + coarse_size * mixed

            @pl.when(turn < last)
            def _():
                g_arrival(turn).wait_recv()
                cur[...] = after + defects[turn]

            @pl.when(turn == last)
            def _():
                c_point[...] = after

            return carry

        lax.fori_loop(1, COARSEN, step, 0)
        point_copy.start()

    @pl.when(both(ends_later, has_group_after))
    def _():
        point_copy.wait_recv()
        c_point[...] = seed_in[...] + defects[last]
        start_copy.start()

    has_start = both(is_last_pos, group > 1)

    @pl.when(has_start)
    def _():
        start_copy.wait_recv()
        g_arrival(1).wait_recv()
        g_turn.start()
        cur[...] = start_in[...]
        chain(0, last, arriving=True)
        corner = own_step()
        residual_ref[0, 0] = corner
        start = start_in[...]
        top_out[...] = corner - start - top_size * mix(start, fine_w.at[0])

    @pl.when(later)
    def _():
        top_copy(0, 0).wait_recv()
        pl.when(is_primary)(lambda: (top_side(0).start(), top_relay().start(), None)[-1])
        top_copy(0, 1).wait_recv()
        pl.when(is_primary)(lambda: top_side(1).start())

        @pl.when(both(is_last_pos, jnp.logical_not(has_start)))
        def _():
            g_arrival(1).wait_recv()
            g_turn.start()

    @pl.when(has_start)
    def _():
        solved = top_in[...]
        top_out[...] = solved + top_size * mix(solved, fine_w.at[0]) + top_out[...]
        pl.when(has_group_after)(send_top)

    @pl.when(later)
    def _():
        cur[...] = top_in[...]
        pl.when(has_start)(lambda: chain(0, last))
        pl.when(jnp.logical_not(has_start))(lambda: chain(0, pos, arriving=True))
        after = own_step()
        states_ref[last, 0] = jnp.where(has_start, top_out[...], after)

        @pl.when(jnp.logical_not(has_start))
        def _():
            residual_ref[0, 0] = after

        @pl.when(both(both(is_last_pos, group == 1), has_group_after))
        def _():
            top_out[...] = after
            send_top()

    @pl.when(opening)
    def _():
        residual_ref[0, 0] = states_ref[last, 0]

    @pl.when(me > 1)
    def _():
        cur[...] = head[...] + fine_size * (head_mix[...] + bias_ref[0])
        states_ref[0, 0] = cur[...]

        def last_sweep(layer, carry):
            after = fine_step(layer)[2]
            cur[...] = after
            states_ref[layer, 0] = after
            return carry

        lax.fori_loop(1, depth - 1, last_sweep, 0)

    @pl.when(both(ends_later, jnp.logical_not(has_group_after)))
    def _():
        point_copy.wait_recv()

    corner = residual_ref[0, 0]
    residual_ref[0, 0] = corner - jnp.where(ends_later, seed_in[...] + defects[last], corner)

    hands_on = both(both(opening, pos == 1), core == 0)

    @pl.when(both(both(opening, pos == 1), core == 1))
    def _():
        seed_copy(last - 1).wait_send()
        open_gate(1)

    @pl.when(hands_on)
    def _():
        pl.semaphore_wait(gate.at[1], 1)
        seed_copy(last - 1).start()

    pl.when(both(has_next, jnp.logical_not(leads)))(first_hop.wait_send)
    pl.when(has_next)(second_hop.wait_send)
    for p in range(1, COARSEN):
        sends_w = both(pos > 0, pos < last) if p == last else pos < 1
        pl.when(both(later, sends_w))(w_copy(p).wait_send)
        pl.when(gives_g(p))(g_copy(p).wait_send)
    pl.when(gives_seed(last))(seed_copy(last).wait_send)
    pl.when(hands_on)(seed_copy(last - 1).wait_send)
    for q in range(last):
        pl.when(holds(q))(y_copy(q).wait_send)
        pl.when(holds(q))(sib_copy(q).wait_send)

    @pl.when(ends_later)
    def _():
        w_turn.wait_send()
        g_turn.wait_send()

    @pl.when(gives_extra)
    def _():
        for index in halves:
            extra_copy(index).wait_send()

    @pl.when(finishes)
    def _():
        for index in halves:
            cross_copy(index).wait_send()

    @pl.when(both(has_group_after, either(finishes, ends_later)))
    def _():
        for p, h in direct:
            top_copy(p, h).wait_send()

    @pl.when(is_primary)
    def _():
        top_relay().wait_send()
        top_side(0).wait_send()
        top_side(1).wait_send()

    pl.when(both(later, pos == 1))(w_ahead.wait_send)

    @pl.when(both(later, pos > 0))
    def _():
        w_back.wait_send()
        pl.when(pos < last)(g_back.wait_send)

    @pl.when(relaxes)
    def _():
        point_copy.wait_send()

    pl.when(both(ends_later, has_group_after))(start_copy.wait_send)


def shards(inputs, guess_states, kernels, biases):
    sections = lax.axis_size("layer")
    depth = guess_states.shape[0]
    state = inputs.shape[1:]
    width = state[-1]
    rows = TAPS * TAPS * width
    vmem = pl.BlockSpec(memory_space=pltpu.VMEM)
    hbm = pl.BlockSpec(memory_space=pltpu.HBM)
    kernel_rows = kernels.reshape(depth, TAPS, rows, width)
    bias_rows = biases.reshape(depth, 1, 1, width)
    f32_state = pltpu.VMEM(state, jnp.float32)
    dma = pltpu.SemaphoreType.DMA
    operands = [pltpu.with_memory_space_constraint(operand, pltpu.HBM)
                for operand in (inputs.reshape(state), guess_states, kernel_rows, bias_rows)]

    def body(*refs):
        cycle_kernel(sections, *refs)

    return tuple(pl.pallas_call(
        body,
        name="mgrit_cycle",
        out_shape=(
            pltpu.VMEM(guess_states.shape, jnp.float32),
            pltpu.VMEM((1,) + guess_states.shape[1:], jnp.float32),
        ),
        in_specs=[hbm, hbm, hbm, hbm],
        out_specs=(vmem, vmem),
        scratch_shapes=[
            f32_state, pltpu.VMEM(bias_rows.shape, jnp.float32),
            pltpu.VMEM((depth, rows, TAPS * width), jnp.bfloat16),
            pltpu.VMEM((COARSEN - 1, rows, TAPS * width), jnp.bfloat16),
            pltpu.VMEM((state[0], state[1] * state[2], rows), jnp.bfloat16),
            f32_state, f32_state, f32_state, f32_state, f32_state, f32_state,
            f32_state, f32_state, f32_state, f32_state, f32_state, f32_state,
            pltpu.VMEM((COARSEN,) + state, jnp.float32),
            dma((depth, TAPS)), dma((2,)), dma((2,)), dma((2,)),
            dma((COARSEN,)), dma((COARSEN - 1,)), dma((COARSEN - 1,)), dma((COARSEN - 1,)),
            dma((COARSEN - 1,)), dma((COARSEN - 1,)), dma((PIECES // 2,)), dma((PIECES // 2,)),
            dma((PIECES // 2,)), dma((PIECES // 2,)), pltpu.SemaphoreType.REGULAR((2,)),
            dma((COARSEN,)), dma((COARSEN,)), dma((COARSEN,)), dma, dma, dma, dma,
            dma((3, 2)), dma((2,)), dma((3,)), dma((2,)), dma((2,)), dma,
        ],
        compiler_params=pltpu.CompilerParams(
            collective_id=0, has_side_effects=True, vmem_limit_bytes=24 * 1024 * 1024),
    )(*operands))


def solution(mesh):
    return jax.shard_map(
        shards,
        mesh=mesh,
        in_specs=(
            P("batch", None, None, None, None),
            P("layer", "batch", None, None, None, None),
            P("layer", None, None, None, None, None),
            P("layer", None),
        ),
        out_specs=(
            P("layer", "batch", None, None, None, None),
            P("layer", "batch", None, None, None, None),
        ),
        check_vma=False,
    )
```

```python
import jax
import jax.numpy as jnp
from jax import lax
from jax.experimental import pallas as pl
from jax.experimental.pallas import tpu as pltpu
from jax.sharding import PartitionSpec as P

COARSEN = 4
TAPS = 3
PIECES = 4
MESH = pl.DeviceIdType.MESH


def cycle_kernel(sections, inputs_hbm, guess_ref, kern_ref, bias_hbm, states_ref, residual_ref,
                 inputs_ref, bias_ref, fine_w, lead_w, patches, cur, head, head_mix,
                 first_head, next_head, corner_out, seed_out, seed_in, c_point,
                 start_in, top_in, top_out, defects,
                 load_sem, small_sem, hop_send, hop_recv, w_send, w_recv, y_send, y_recv, sib_send, sib_recv,
                 extra_send, extra_recv, cross_send, cross_recv, gate,
                 g_send, g_recv, seed_send, seed_recv, origin_send, start_send, start_recv, top_send, top_recv, relay_send, turn_send, back_send, ahead_send):
    depth = guess_ref.shape[0]
    size_x, size_y, size_z, width = inputs_ref.shape
    groups = sections // COARSEN
    fine_size = 2.0 / (depth * sections)
    coarse_size = depth * fine_size
    top_size = COARSEN * coarse_size
    rows = TAPS * TAPS * width
    piece_rows = rows // PIECES
    last = COARSEN - 1
    extra = COARSEN - 2
    span = COARSEN // 2
    me = lax.axis_index("layer")
    part = lax.axis_index("batch")
    pos = lax.rem(me, COARSEN)
    group = me // COARSEN
    core = lax.rem(part, 2)
    row = lax.rem(part // 2, 2)
    sibling = part + 1 - 2 * core
    across = part + 2 - 4 * row
    both = jnp.logical_and
    either = jnp.logical_or
    is_first = me == 0
    has_next = me < sections - 1
    later = group > 0
    opening = group == 0
    has_group_after = group < groups - 1
    is_last_pos = pos == last
    is_upper = pos >= last - 1

    def device(p, ahead=0):
        return ((group + ahead) * COARSEN + p, part)

    barrier = pltpu.get_barrier_semaphore()

    def greet(target):
        pl.semaphore_signal(barrier, inc=1, device_id=target, device_id_type=MESH)

    for rel in range(1, COARSEN):
        greet(device(lax.rem(pos + rel, COARSEN)))
    greet((me, sibling))
    greet((me, across))
    greets_ahead = both(is_upper, has_group_after)

    @pl.when(greets_ahead)
    def _():
        for p in range(COARSEN):
            greet(device(p, 1))

    @pl.when(later)
    def _():
        for p in (last - 1, last):
            greet(device(p, -1))

    def fine_load(layer, tap):
        return pltpu.make_async_copy(
            kern_ref.at[layer, tap],
            fine_w.at[layer, :, pl.ds(tap * width, width)],
            load_sem.at[layer, tap],
        )

    inputs_load = pltpu.make_async_copy(inputs_hbm, inputs_ref, small_sem.at[0])
    bias_load = pltpu.make_async_copy(bias_hbm, bias_ref, small_sem.at[1])
    inputs_load.start()
    bias_load.start()
    for layer in range(depth):
        for tap in range(TAPS):
            fine_load(layer, tap).start()

    greetings = COARSEN + 1 + jnp.where(greets_ahead, COARSEN, 0) + jnp.where(later, 2, 0)
    pl.semaphore_wait(barrier, greetings)

    def remote(source, target, send_sem, recv_sem, where):
        return pltpu.make_async_remote_copy(
            src_ref=source, dst_ref=target, send_sem=send_sem, recv_sem=recv_sem,
            device_id=where, device_id_type=MESH)

    def hop(index, source, target):
        return remote(source, target, hop_send.at[index], hop_recv.at[index], (me + 1, part))

    first_hop = hop(0, guess_ref.at[depth - 1, 0], first_head)
    second_hop = hop(1, corner_out, next_head)
    staggers = both(has_next, me < 2)
    leads = both(staggers, core == jnp.where(me == 1, 1, 0))
    trails = both(staggers, jnp.logical_not(leads))
    waits_loads = both(core == 1, me > 1)
    pl.when(both(has_next, jnp.logical_not(either(trails, waits_loads))))(first_hop.start)

    def open_gate(index):
        pl.semaphore_signal(gate.at[index], inc=1, device_id=(me, sibling), device_id_type=MESH)


    slot = jnp.minimum(pos, last - 1)
    quarter = pl.ds(pl.multiple_of((core * 2 + row) * piece_rows, 16), piece_rows)
    half = pl.ds(pl.multiple_of(core * 2 * piece_rows, 16), 2 * piece_rows)

    def w_copy(p):
        return remote(fine_w.at[0, quarter], lead_w.at[slot, quarter], w_send.at[p], w_recv.at[slot], device(p))

    def w_arrival(q):
        return remote(lead_w.at[q, quarter], lead_w.at[q, quarter], w_send.at[0], w_recv.at[q], device(q))

    w_turn = remote(lead_w.at[1, quarter], lead_w.at[1, quarter], turn_send.at[0], w_recv.at[1], device(last - 1))

    def y_copy(q):
        return remote(lead_w.at[q, quarter], lead_w.at[q, quarter], y_send.at[q], y_recv.at[q], (me, across))

    def sib_copy(q):
        return remote(lead_w.at[q, half], lead_w.at[q, half], sib_send.at[q], sib_recv.at[q], (me, sibling))

    def extra_copy(index):
        piece = pl.ds(pl.multiple_of((row * 2 + index) * piece_rows, 16), piece_rows)
        return remote(fine_w.at[0, piece], lead_w.at[extra, piece], extra_send.at[index], extra_recv.at[index],
                      device(2 * last - 1 - pos))

    def cross_copy(index):
        piece = pl.ds(pl.multiple_of((row * 2 + index) * piece_rows, 16), piece_rows)
        return remote(lead_w.at[extra, piece], lead_w.at[extra, piece], cross_send.at[index], cross_recv.at[index],
                      (me, across))

    gives_extra = both(opening, either(both(pos == last - 1, core == 0), both(pos == last, core == 1)))
    finishes = both(opening, either(both(pos == last, core == 0), both(pos == last - 1, core == 1)))

    def send_w(source, targets):
        @pl.when(both(later, pos == source))
        def _():
            for p in targets:
                w_copy(p).start()

    halves = range(PIECES // 2)

    def send_extra(source):
        @pl.when(both(gives_extra, pos == source))
        def _():
            for index in halves:
                extra_copy(index).start()

    def pass_extra(target):
        @pl.when(both(finishes, pos == target))
        def _():
            for index in halves:
                extra_copy(index).wait_recv()
                cross_copy(index).start()

    w_ahead = remote(lead_w.at[0, quarter], lead_w.at[0, quarter], ahead_send, w_recv.at[0], device(last))
    back_slot = jnp.maximum(pos - 1, 0)
    w_back = remote(fine_w.at[0, quarter], lead_w.at[back_slot, quarter], back_send.at[0], w_recv.at[back_slot], device(0))

    def send_back(sources):
        for source in sources:
            pl.when(both(later, pos == source))(w_back.start)

    def holds(q):
        return both(later, either(pos > q, pos == 0))

    def first_wave():
        send_w(0, (2, 1))
        send_w(1, (3,))
        send_w(2, (3,))
        send_back((1, 2))

    def pass_w(target, qs):
        @pl.when(both(later, pos == target))
        def _():
            for q in qs:
                w_arrival(q).wait_recv()
                y_copy(q).start()
                if target == last and q == 1:
                    w_turn.start()

    for tap in range(TAPS):
        fine_load(0, tap).wait()
    send_extra(last - 1)
    inputs_load.wait()
    bias_load.wait()
    for layer in range(1, depth):
        for tap in range(TAPS):
            fine_load(layer, tap).wait()
    pl.when(both(has_next, waits_loads))(first_hop.start)
    send_extra(last)

    def let_pass():
        first_hop.wait_send()
        open_gate(0)

    def follow():
        pl.semaphore_wait(gate.at[0], 1)
        first_hop.start()

    first_wave()
    pl.when(both(leads, me > 0))(let_pass)
    pl.when(both(trails, me > 0))(follow)

    z_index = lax.broadcasted_iota(jnp.int32, (size_x * size_y, size_z, width), 1)

    def mix(state, weights):
        squashed = jnp.tanh(state).reshape(size_x * size_y, size_z, width)
        below = jnp.where(z_index == 0, 0.0, pltpu.roll(squashed, 1, 1))
        above = jnp.where(z_index == size_z - 1, 0.0, pltpu.roll(squashed, size_z - 1, 1))
        span = size_y * size_z
        edge = jnp.zeros((size_x, size_z, width), jnp.float32)
        for tap_z, shifted in enumerate((below, squashed, above)):
            shifted = shifted.reshape(size_x, span, width)
            even = shifted.astype(jnp.bfloat16)
            odd = jnp.concatenate([edge, shifted, edge], 1).astype(jnp.bfloat16)
            for tap_y, block in enumerate((odd[:, :span], even, odd[:, 2 * size_z:])):
                column = (tap_y * TAPS + tap_z) * width
                patches[:, :, column:column + width] = block
        left = patches[...].reshape(size_x * span, rows)
        product = jnp.dot(left, weights[...], preferred_element_type=jnp.float32)
        product = product.reshape(size_x, size_y, size_z, TAPS * width)
        plane = jnp.zeros((1, size_y, size_z, width), jnp.float32)
        total = product[..., width:2 * width]
        total = total + jnp.concatenate([plane, product[:-1, :, :, :width]], 0)
        return total + jnp.concatenate([product[1:, :, :, 2 * width:], plane], 0)

    def fine_step(layer):
        state = cur[...]
        mixed = mix(state, fine_w.at[layer])
        return state, mixed, state + fine_size * (mixed + bias_ref[layer])

    pl.when(me > 0)(first_hop.wait_recv)
    cur[...] = jnp.where(is_first, inputs_ref[...], first_head[...])

    def sweep_one(layer, carry):
        after = fine_step(layer)[2]
        cur[...] = after
        states_ref[layer, 0] = after
        pl.when(both(both(leads, is_first), layer == depth - 2))(let_pass)
        pl.when(both(both(trails, is_first), layer == depth - 2))(follow)
        return carry

    lax.fori_loop(0, depth, sweep_one, 0)
    corner_out[...] = cur[...]
    pl.when(has_next)(second_hop.start)
    pass_extra(last)
    pass_w(0, (1, 0))
    pass_w(1, (0,))
    pass_w(2, (0,))
    pass_w(3, (1, 2))

    def seed_copy(p):
        return remote(seed_out, seed_in, seed_send.at[p], seed_recv, device(p))

    def gives_seed(p):
        exact = both(opening, pos == 1)
        if p == last:
            handed = both(opening, both(pos == 2, core == 1))
            return either(both(exact, core == 0), handed)
        return exact

    takes_seed = either(is_last_pos, both(opening, pos == last - 1))

    def g_copy(p):
        return remote(defects.at[pos], defects.at[pos], g_send.at[p], g_recv.at[pos], device(p))

    def g_arrival(q):
        return remote(defects.at[q], defects.at[q], g_send.at[0], g_recv.at[q], device(q))

    def gives_g(p):
        if p == last:
            return both(pos < p, either(later, both(pos == last - 1, core == 0)))
        ahead = both(pos < (1 if p == last - 1 else p), later)
        return either(ahead, both(opening, both(is_last_pos, core == 1))) if p == last - 1 else ahead

    @pl.when(me > 0)
    def _():
        second_hop.wait_recv()
        pl.when(both(later, pos == 1))(w_ahead.start)
        send_back((3,))
        pass_extra(last - 1)
        head[...] = next_head[...]
        cur[...] = next_head[...]

        def sweep_two(layer, carry):
            _, mixed, after = fine_step(layer)

            @pl.when(layer == 0)
            def _():
                head_mix[...] = mixed

            cur[...] = after
            states_ref[layer, 0] = after
            return carry

        lax.fori_loop(0, depth, sweep_two, 0)

        @pl.when(opening)
        def _():
            seed_out[...] = cur[...]
            pl.when(both(gives_seed(last), pos == 1))(seed_copy(last).start)
            pl.when(both(gives_seed(last - 1), core == 1))(seed_copy(last - 1).start)

        defects[pos] = cur[...] - head[...] - coarse_size * head_mix[...]
        for p in (last, last - 1, 1):
            pl.when(gives_g(p))(g_copy(p).start)

    g_turn = remote(defects.at[1], defects.at[1], turn_send.at[1], g_recv.at[1], device(last - 1))

    g_back = remote(defects.at[pos], defects.at[pos], back_send.at[1], g_recv.at[pos], device(0))
    pl.when(both(later, both(pos > 0, pos < last)))(g_back.start)
    pass_w(2, (1,))
    pass_w(3, (0,))
    pass_w(0, (2,))


    for q in range(last):
        @pl.when(both(later, either(pos > q, both(pos == 0, q < last - 1))))
        def _(q=q):
            y_copy(q).wait_recv()
            sib_copy(q).start()

    ends_later = both(is_last_pos, later)
    def own_step():
        state = cur[...]
        mixed = mix(state, fine_w.at[0])
        head[...] = state
        head_mix[...] = mixed
        return state + coarse_size * mixed + defects[pos]

    def chain(low, high, arriving=False):
        def step(turn, carry):
            state = cur[...]
            if arriving:
                sib_copy(turn).wait_recv()
            mixed = mix(state, lead_w.at[turn])
            if arriving:
                pl.when(jnp.logical_not(both(is_last_pos, turn == 1)))(g_arrival(turn).wait_recv)
            cur[...] = state + coarse_size * mixed + defects[turn]
            return carry

        lax.fori_loop(low, high, step, 0)

    def extra_step(q):
        state = cur[...]
        for index in halves:
            cross_copy(index).wait_recv()
        mixed = mix(state, lead_w.at[extra])
        g_arrival(q).wait_recv()
        cur[...] = state + coarse_size * mixed + defects[q]

    half_planes = size_x // 2
    direct = [(0, 0), (0, 1), (2, 0), (2, 1), (1, 1)]
    targets = (last - core, last - span - core, core)

    def top_copy(p, h):
        planes = pl.ds(h * half_planes, half_planes)
        return remote(top_out.at[planes], top_in.at[planes], top_send.at[p, h], top_recv.at[h], device(targets[p], 1))

    def top_relay():
        planes = pl.ds(0, half_planes)
        return remote(top_in.at[planes], top_in.at[planes], relay_send.at[0], top_recv.at[0], device(pos - span))

    def top_side(h):
        planes = pl.ds(h * half_planes, half_planes)
        return remote(top_in.at[planes], top_in.at[planes], relay_send.at[h + 1], top_recv.at[h],
                      device(2 * last - 1 - pos))

    is_primary = both(later, pos == last - core)

    def send_top():
        for p, h in direct:
            top_copy(p, h).start()

    start_copy = remote(c_point, start_in, start_send, start_recv, device(last, 1))

    @pl.when(both(opening, is_upper))
    def _():
        seed_copy(0).wait_recv()
        cur[...] = seed_in[...]

        @pl.when(both(is_last_pos, finishes))
        def _():
            extra_step(last - 1)

        after = own_step()
        states_ref[last, 0] = after
        cur[...] = after

        @pl.when(both(pos == last - 1, finishes))
        def _():
            seed_out[...] = after
            seed_copy(last).start()
            extra_step(last)

        @pl.when(both(finishes, has_group_after))
        def _():
            top_out[...] = cur[...]
            send_top()

    relaxes = both(later, pos == 0)
    point_copy = remote(c_point, seed_in, origin_send, seed_recv, device(last))

    @pl.when(relaxes)
    def _():
        def step(turn, carry):
            state = cur[...]
            sib_copy(turn - 1).wait_recv()
            mixed = mix(state, lead_w.at[turn - 1])

            @pl.when(turn == last - 1)
            def _():
                y_copy(last - 1).wait_recv()
                sib_copy(last - 1).start()

            after = state + coarse_size * mixed

            @pl.when(turn < last)
            def _():
                g_arrival(turn).wait_recv()
                cur[...] = after + defects[turn]

            @pl.when(turn == last)
            def _():
                c_point[...] = after

            return carry

        lax.fori_loop(1, COARSEN, step, 0)
        point_copy.start()

    @pl.when(both(ends_later, has_group_after))
    def _():
        point_copy.wait_recv()
        c_point[...] = seed_in[...] + defects[last]
        start_copy.start()

    has_start = both(is_last_pos, group > 1)

    @pl.when(has_start)
    def _():
        start_copy.wait_recv()
        g_arrival(1).wait_recv()
        g_turn.start()
        cur[...] = start_in[...]
        chain(0, last, arriving=True)
        corner = own_step()
        residual_ref[0, 0] = corner
        start = start_in[...]
        top_out[...] = corner - start - top_size * mix(start, fine_w.at[0])

    @pl.when(later)
    def _():
        @pl.when(both(jnp.logical_not(is_primary), both(is_last_pos, jnp.logical_not(has_start))))
        def _():
            g_arrival(1).wait_recv()
            g_turn.start()

        top_copy(0, 0).wait_recv()
        pl.when(is_primary)(lambda: (top_side(0).start(), top_relay().start(), None)[-1])
        top_copy(0, 1).wait_recv()
        pl.when(is_primary)(lambda: top_side(1).start())

        @pl.when(both(is_primary, both(is_last_pos, jnp.logical_not(has_start))))
        def _():
            g_arrival(1).wait_recv()
            g_turn.start()

    @pl.when(has_start)
    def _():
        solved = top_in[...]
        top_out[...] = solved + top_size * mix(solved, fine_w.at[0]) + top_out[...]
        pl.when(has_group_after)(send_top)

    @pl.when(later)
    def _():
        cur[...] = top_in[...]
        pl.when(has_start)(lambda: chain(0, last))
        pl.when(jnp.logical_not(has_start))(lambda: chain(0, pos, arriving=True))
        after = own_step()
        states_ref[last, 0] = jnp.where(has_start, top_out[...], after)

        @pl.when(jnp.logical_not(has_start))
        def _():
            residual_ref[0, 0] = after

        @pl.when(both(both(is_last_pos, group == 1), has_group_after))
        def _():
            top_out[...] = after
            send_top()

    @pl.when(opening)
    def _():
        residual_ref[0, 0] = states_ref[last, 0]

    @pl.when(me > 1)
    def _():
        cur[...] = head[...] + fine_size * (head_mix[...] + bias_ref[0])
        states_ref[0, 0] = cur[...]

        def last_sweep(layer, carry):
            after = fine_step(layer)[2]
            cur[...] = after
            states_ref[layer, 0] = after
            return carry

        lax.fori_loop(1, depth - 1, last_sweep, 0)

    @pl.when(both(ends_later, jnp.logical_not(has_group_after)))
    def _():
        point_copy.wait_recv()

    corner = residual_ref[0, 0]
    residual_ref[0, 0] = corner - jnp.where(ends_later, seed_in[...] + defects[last], corner)

    hands_on = both(both(opening, pos == 1), core == 0)

    @pl.when(both(both(opening, pos == 1), core == 1))
    def _():
        seed_copy(last - 1).wait_send()
        open_gate(1)

    @pl.when(hands_on)
    def _():
        pl.semaphore_wait(gate.at[1], 1)
        seed_copy(last - 1).start()

    pl.when(both(has_next, jnp.logical_not(leads)))(first_hop.wait_send)
    pl.when(has_next)(second_hop.wait_send)
    for p in range(1, COARSEN):
        sends_w = both(pos > 0, pos < last) if p == last else pos < 1
        pl.when(both(later, sends_w))(w_copy(p).wait_send)
        pl.when(gives_g(p))(g_copy(p).wait_send)
    pl.when(gives_seed(last))(seed_copy(last).wait_send)
    pl.when(hands_on)(seed_copy(last - 1).wait_send)
    for q in range(last):
        pl.when(holds(q))(y_copy(q).wait_send)
        pl.when(holds(q))(sib_copy(q).wait_send)

    @pl.when(ends_later)
    def _():
        w_turn.wait_send()
        g_turn.wait_send()

    @pl.when(gives_extra)
    def _():
        for index in halves:
            extra_copy(index).wait_send()

    @pl.when(finishes)
    def _():
        for index in halves:
            cross_copy(index).wait_send()

    @pl.when(both(has_group_after, either(finishes, ends_later)))
    def _():
        for p, h in direct:
            top_copy(p, h).wait_send()

    @pl.when(is_primary)
    def _():
        top_relay().wait_send()
        top_side(0).wait_send()
        top_side(1).wait_send()

    pl.when(both(later, pos == 1))(w_ahead.wait_send)

    @pl.when(both(later, pos > 0))
    def _():
        w_back.wait_send()
        pl.when(pos < last)(g_back.wait_send)

    @pl.when(relaxes)
    def _():
        point_copy.wait_send()

    pl.when(both(ends_later, has_group_after))(start_copy.wait_send)


def shards(inputs, guess_states, kernels, biases):
    sections = lax.axis_size("layer")
    depth = guess_states.shape[0]
    state = inputs.shape[1:]
    width = state[-1]
    rows = TAPS * TAPS * width
    vmem = pl.BlockSpec(memory_space=pltpu.VMEM)
    hbm = pl.BlockSpec(memory_space=pltpu.HBM)
    kernel_rows = kernels.reshape(depth, TAPS, rows, width)
    bias_rows = biases.reshape(depth, 1, 1, width)
    f32_state = pltpu.VMEM(state, jnp.float32)
    dma = pltpu.SemaphoreType.DMA
    operands = [pltpu.with_memory_space_constraint(operand, pltpu.HBM)
                for operand in (inputs.reshape(state), guess_states, kernel_rows, bias_rows)]

    def body(*refs):
        cycle_kernel(sections, *refs)

    return tuple(pl.pallas_call(
        body,
        name="mgrit_cycle",
        out_shape=(
            pltpu.VMEM(guess_states.shape, jnp.float32),
            pltpu.VMEM((1,) + guess_states.shape[1:], jnp.float32),
        ),
        in_specs=[hbm, hbm, hbm, hbm],
        out_specs=(vmem, vmem),
        scratch_shapes=[
            f32_state, pltpu.VMEM(bias_rows.shape, jnp.float32),
            pltpu.VMEM((depth, rows, TAPS * width), jnp.bfloat16),
            pltpu.VMEM((COARSEN - 1, rows, TAPS * width), jnp.bfloat16),
            pltpu.VMEM((state[0], state[1] * state[2], rows), jnp.bfloat16),
            f32_state, f32_state, f32_state, f32_state, f32_state, f32_state,
            f32_state, f32_state, f32_state, f32_state, f32_state, f32_state,
            pltpu.VMEM((COARSEN,) + state, jnp.float32),
            dma((depth, TAPS)), dma((2,)), dma((2,)), dma((2,)),
            dma((COARSEN,)), dma((COARSEN - 1,)), dma((COARSEN - 1,)), dma((COARSEN - 1,)),
            dma((COARSEN - 1,)), dma((COARSEN - 1,)), dma((PIECES // 2,)), dma((PIECES // 2,)),
            dma((PIECES // 2,)), dma((PIECES // 2,)), pltpu.SemaphoreType.REGULAR((2,)),
            dma((COARSEN,)), dma((COARSEN,)), dma((COARSEN,)), dma, dma, dma, dma,
            dma((3, 2)), dma((2,)), dma((3,)), dma((2,)), dma((2,)), dma,
        ],
        compiler_params=pltpu.CompilerParams(
            collective_id=0, has_side_effects=True, vmem_limit_bytes=24 * 1024 * 1024),
    )(*operands))


def solution(mesh):
    return jax.shard_map(
        shards,
        mesh=mesh,
        in_specs=(
            P("batch", None, None, None, None),
            P("layer", "batch", None, None, None, None),
            P("layer", None, None, None, None, None),
            P("layer", None),
        ),
        out_specs=(
            P("layer", "batch", None, None, None, None),
            P("layer", "batch", None, None, None, None),
        ),
        check_vma=False,
    )
```

```python
import jax
import jax.numpy as jnp
from jax import lax
from jax.experimental import pallas as pl
from jax.experimental.pallas import tpu as pltpu
from jax.sharding import PartitionSpec as P

COARSEN = 4
TAPS = 3
PIECES = 4
MESH = pl.DeviceIdType.MESH


def cycle_kernel(sections, inputs_hbm, guess_ref, kern_ref, bias_hbm, states_ref, residual_ref,
                 inputs_ref, bias_ref, own_w, fine_w, lead_w, patches, cur, head, head_mix,
                 first_head, next_head, corner_out, seed_out, seed_in, c_point,
                 start_in, top_in, top_out, defects,
                 own_sem, load_sem, small_sem, hop_send, hop_recv, w_send, w_recv, y_send, y_recv, sib_send, sib_recv,
                 extra_send, extra_recv, cross_send, cross_recv, gate,
                 g_send, g_recv, seed_send, seed_recv, origin_send, start_send, start_recv, top_send, top_recv, relay_send, turn_send, back_send, ahead_send):
    depth = guess_ref.shape[0]
    size_x, size_y, size_z, width = inputs_ref.shape
    groups = sections // COARSEN
    fine_size = 2.0 / (depth * sections)
    coarse_size = depth * fine_size
    top_size = COARSEN * coarse_size
    rows = TAPS * TAPS * width
    piece_rows = rows // PIECES
    tap_rows = TAPS * width
    far_rows = 2 * tap_rows
    last = COARSEN - 1
    extra = COARSEN - 2
    span = COARSEN // 2
    me = lax.axis_index("layer")
    part = lax.axis_index("batch")
    pos = lax.rem(me, COARSEN)
    group = me // COARSEN
    core = lax.rem(part, 2)
    row = lax.rem(part // 2, 2)
    sibling = part + 1 - 2 * core
    across = part + 2 - 4 * row
    both = jnp.logical_and
    either = jnp.logical_or
    is_first = me == 0
    has_next = me < sections - 1
    later = group > 0
    opening = group == 0
    has_group_after = group < groups - 1
    is_last_pos = pos == last
    is_upper = pos >= last - 1

    def device(p, ahead=0):
        return ((group + ahead) * COARSEN + p, part)

    barrier = pltpu.get_barrier_semaphore()

    def greet(target):
        pl.semaphore_signal(barrier, inc=1, device_id=target, device_id_type=MESH)

    for rel in range(1, COARSEN):
        greet(device(lax.rem(pos + rel, COARSEN)))
    greet((me, sibling))
    greet((me, across))
    greets_ahead = both(is_upper, has_group_after)

    @pl.when(greets_ahead)
    def _():
        for p in range(COARSEN):
            greet(device(p, 1))

    @pl.when(later)
    def _():
        for p in (last - 1, last):
            greet(device(p, -1))

    def own_load(tap):
        return pltpu.make_async_copy(
            kern_ref.at[0, tap], own_w.at[:, pl.ds(tap * width, width)], own_sem.at[tap])

    parts = ((0, 0, rows, 0, 0), (1, 0, rows, 0, width),
             (2, 0, far_rows, rows, 0), (2, far_rows, tap_rows, rows + tap_rows, width))

    def fine_load(layer, index):
        tap, start, count, place, column = parts[index]
        return pltpu.make_async_copy(
            kern_ref.at[layer, tap, pl.ds(start, count)],
            fine_w.at[layer - 1, pl.ds(place, count), pl.ds(column, width)],
            load_sem.at[layer - 1, index],
        )

    inputs_load = pltpu.make_async_copy(inputs_hbm, inputs_ref, small_sem.at[0])
    bias_load = pltpu.make_async_copy(bias_hbm, bias_ref, small_sem.at[1])
    inputs_load.start()
    bias_load.start()
    for tap in range(TAPS):
        own_load(tap).start()
    for layer in range(1, depth):
        for index in range(len(parts)):
            fine_load(layer, index).start()
    fine_w[:, rows:rows + tap_rows, width:] = jnp.zeros((depth - 1, tap_rows, width), jnp.bfloat16)

    greetings = COARSEN + 1 + jnp.where(greets_ahead, COARSEN, 0) + jnp.where(later, 2, 0)
    pl.semaphore_wait(barrier, greetings)

    def remote(source, target, send_sem, recv_sem, where):
        return pltpu.make_async_remote_copy(
            src_ref=source, dst_ref=target, send_sem=send_sem, recv_sem=recv_sem,
            device_id=where, device_id_type=MESH)

    def hop(index, source, target):
        return remote(source, target, hop_send.at[index], hop_recv.at[index], (me + 1, part))

    first_hop = hop(0, guess_ref.at[depth - 1, 0], first_head)
    second_hop = hop(1, corner_out, next_head)
    staggers = both(has_next, me < 2)
    leads = both(staggers, core == jnp.where(me == 1, 1, 0))
    trails = both(staggers, jnp.logical_not(leads))
    waits_loads = both(core == 1, me > 1)
    pl.when(both(has_next, jnp.logical_not(either(trails, waits_loads))))(first_hop.start)

    def open_gate(index):
        pl.semaphore_signal(gate.at[index], inc=1, device_id=(me, sibling), device_id_type=MESH)


    slot = jnp.minimum(pos, last - 1)
    quarter = pl.ds(pl.multiple_of((core * 2 + row) * piece_rows, 16), piece_rows)
    half = pl.ds(pl.multiple_of(core * 2 * piece_rows, 16), 2 * piece_rows)

    def w_copy(p):
        return remote(own_w.at[quarter], lead_w.at[slot, quarter], w_send.at[p], w_recv.at[slot], device(p))

    def w_arrival(q):
        return remote(lead_w.at[q, quarter], lead_w.at[q, quarter], w_send.at[0], w_recv.at[q], device(q))

    w_turn = remote(lead_w.at[1, quarter], lead_w.at[1, quarter], turn_send.at[0], w_recv.at[1], device(last - 1))

    def y_copy(q):
        return remote(lead_w.at[q, quarter], lead_w.at[q, quarter], y_send.at[q], y_recv.at[q], (me, across))

    def sib_copy(q):
        return remote(lead_w.at[q, half], lead_w.at[q, half], sib_send.at[q], sib_recv.at[q], (me, sibling))

    def extra_copy(index):
        piece = pl.ds(pl.multiple_of((row * 2 + index) * piece_rows, 16), piece_rows)
        return remote(own_w.at[piece], lead_w.at[extra, piece], extra_send.at[index], extra_recv.at[index],
                      device(2 * last - 1 - pos))

    def cross_copy(index):
        piece = pl.ds(pl.multiple_of((row * 2 + index) * piece_rows, 16), piece_rows)
        return remote(lead_w.at[extra, piece], lead_w.at[extra, piece], cross_send.at[index], cross_recv.at[index],
                      (me, across))

    gives_extra = both(opening, either(both(pos == last - 1, core == 0), both(pos == last, core == 1)))
    finishes = both(opening, either(both(pos == last, core == 0), both(pos == last - 1, core == 1)))

    def send_w(source, targets):
        @pl.when(both(later, pos == source))
        def _():
            for p in targets:
                w_copy(p).start()

    halves = range(PIECES // 2)

    def send_extra(source):
        @pl.when(both(gives_extra, pos == source))
        def _():
            for index in halves:
                extra_copy(index).start()

    def pass_extra(target):
        @pl.when(both(finishes, pos == target))
        def _():
            for index in halves:
                extra_copy(index).wait_recv()
                cross_copy(index).start()

    w_ahead = remote(lead_w.at[0, quarter], lead_w.at[0, quarter], ahead_send, w_recv.at[0], device(last))
    back_slot = jnp.maximum(pos - 1, 0)
    w_back = remote(own_w.at[quarter], lead_w.at[back_slot, quarter], back_send.at[0], w_recv.at[back_slot], device(0))

    def send_back(sources):
        for source in sources:
            pl.when(both(later, pos == source))(w_back.start)

    def holds(q):
        return both(later, either(pos > q, pos == 0))

    def first_wave():
        send_w(0, (2, 1))
        send_w(1, (3,))
        send_w(2, (3,))
        send_back((1, 2))

    def pass_w(target, qs):
        @pl.when(both(later, pos == target))
        def _():
            for q in qs:
                w_arrival(q).wait_recv()
                y_copy(q).start()
                if target == last and q == 1:
                    w_turn.start()

    for tap in range(TAPS):
        own_load(tap).wait()
    send_extra(last - 1)
    inputs_load.wait()
    bias_load.wait()
    for layer in range(1, depth):
        for index in range(len(parts)):
            fine_load(layer, index).wait()
    pl.when(both(has_next, waits_loads))(first_hop.start)
    send_extra(last)

    def let_pass():
        first_hop.wait_send()
        open_gate(0)

    def follow():
        pl.semaphore_wait(gate.at[0], 1)
        first_hop.start()

    first_wave()
    pl.when(both(leads, me > 0))(let_pass)
    pl.when(both(trails, me > 0))(follow)

    z_index = lax.broadcasted_iota(jnp.int32, (size_x * size_y, size_z, width), 1)

    def gather(state):
        squashed = jnp.tanh(state).reshape(size_x * size_y, size_z, width)
        below = jnp.where(z_index == 0, 0.0, pltpu.roll(squashed, 1, 1))
        above = jnp.where(z_index == size_z - 1, 0.0, pltpu.roll(squashed, size_z - 1, 1))
        span = size_y * size_z
        edge = jnp.zeros((size_x, size_z, width), jnp.float32)
        for tap_z, shifted in enumerate((below, squashed, above)):
            shifted = shifted.reshape(size_x, span, width)
            even = shifted.astype(jnp.bfloat16)
            odd = jnp.concatenate([edge, shifted, edge], 1).astype(jnp.bfloat16)
            for tap_y, block in enumerate((odd[:, :span], even, odd[:, 2 * size_z:])):
                column = (tap_y * TAPS + tap_z) * width
                patches[:, :, column:column + width] = block
        return patches[...].reshape(size_x * span, rows)

    def mix(state, weights):
        left = gather(state)
        product = jnp.dot(left, weights[...], preferred_element_type=jnp.float32)
        product = product.reshape(size_x, size_y, size_z, TAPS * width)
        plane = jnp.zeros((1, size_y, size_z, width), jnp.float32)
        total = product[..., width:2 * width]
        total = total + jnp.concatenate([plane, product[:-1, :, :, :width]], 0)
        return total + jnp.concatenate([product[1:, :, :, 2 * width:], plane], 0)

    def packed_mix(state, weights):
        left = gather(state)
        near = jnp.dot(left, weights[:rows], preferred_element_type=jnp.float32)
        far = jnp.dot(left[:, :far_rows], weights[rows:], preferred_element_type=jnp.float32)
        near = near.reshape(size_x, size_y, size_z, 2 * width)
        far = far.reshape(size_x, size_y, size_z, 2 * width)
        plane = jnp.zeros((1, size_y, size_z, width), jnp.float32)
        line = jnp.zeros((size_x - 1, 1, size_z, width), jnp.float32)
        ahead = far[1:, :, :, :width] + jnp.concatenate([far[1:, 1:, :, width:], line], 1)
        total = near[..., width:]
        total = total + jnp.concatenate([plane, near[:-1, :, :, :width]], 0)
        return total + jnp.concatenate([ahead, plane], 0)

    def fine_step(layer, lead=False):
        state = cur[...]
        mixed = mix(state, own_w) if lead else packed_mix(state, fine_w.at[layer - 1])
        return state, mixed, state + fine_size * (mixed + bias_ref[layer])

    pl.when(me > 0)(first_hop.wait_recv)
    cur[...] = jnp.where(is_first, inputs_ref[...], first_head[...])

    def sweep_one(layer, carry, lead=False):
        after = fine_step(layer, lead)[2]
        cur[...] = after
        states_ref[layer, 0] = after
        pl.when(both(both(leads, is_first), layer == depth - 2))(let_pass)
        pl.when(both(both(trails, is_first), layer == depth - 2))(follow)
        return carry

    sweep_one(0, 0, True)
    lax.fori_loop(1, depth, sweep_one, 0)
    corner_out[...] = cur[...]
    pl.when(has_next)(second_hop.start)
    pass_extra(last)
    pass_w(0, (1, 0))
    pass_w(1, (0,))
    pass_w(2, (0,))
    pass_w(3, (1, 2))

    def seed_copy(p):
        return remote(seed_out, seed_in, seed_send.at[p], seed_recv, device(p))

    def gives_seed(p):
        exact = both(opening, pos == 1)
        if p == last:
            handed = both(opening, both(pos == 2, core == 1))
            return either(both(exact, core == 0), handed)
        return exact

    takes_seed = either(is_last_pos, both(opening, pos == last - 1))

    def g_copy(p):
        return remote(defects.at[pos], defects.at[pos], g_send.at[p], g_recv.at[pos], device(p))

    def g_arrival(q):
        return remote(defects.at[q], defects.at[q], g_send.at[0], g_recv.at[q], device(q))

    def gives_g(p):
        if p == last:
            return both(pos < p, either(later, both(pos == last - 1, core == 0)))
        ahead = both(pos < (1 if p == last - 1 else p), later)
        return either(ahead, both(opening, both(is_last_pos, core == 1))) if p == last - 1 else ahead

    @pl.when(me > 0)
    def _():
        second_hop.wait_recv()
        pl.when(both(later, pos == 1))(w_ahead.start)
        send_back((3,))
        pass_extra(last - 1)
        head[...] = next_head[...]
        cur[...] = next_head[...]

        def sweep_two(layer, carry, lead=False):
            _, mixed, after = fine_step(layer, lead)
            if lead:
                head_mix[...] = mixed
            cur[...] = after
            states_ref[layer, 0] = after
            return carry

        sweep_two(0, 0, True)
        lax.fori_loop(1, depth, sweep_two, 0)

        @pl.when(opening)
        def _():
            seed_out[...] = cur[...]
            pl.when(both(gives_seed(last), pos == 1))(seed_copy(last).start)
            pl.when(both(gives_seed(last - 1), core == 1))(seed_copy(last - 1).start)

        defects[pos] = cur[...] - head[...] - coarse_size * head_mix[...]
        for p in (last, last - 1, 1):
            pl.when(gives_g(p))(g_copy(p).start)

    g_turn = remote(defects.at[1], defects.at[1], turn_send.at[1], g_recv.at[1], device(last - 1))

    g_back = remote(defects.at[pos], defects.at[pos], back_send.at[1], g_recv.at[pos], device(0))
    pl.when(both(later, both(pos > 0, pos < last)))(g_back.start)
    pass_w(2, (1,))
    pass_w(3, (0,))
    pass_w(0, (2,))


    for q in range(last):
        @pl.when(both(later, either(pos > q, both(pos == 0, q < last - 1))))
        def _(q=q):
            y_copy(q).wait_recv()
            sib_copy(q).start()

    ends_later = both(is_last_pos, later)
    def own_step():
        state = cur[...]
        mixed = mix(state, own_w)
        head[...] = state
        head_mix[...] = mixed
        return state + coarse_size * mixed + defects[pos]

    def chain(low, high, arriving=False):
        def step(turn, carry):
            state = cur[...]
            if arriving:
                sib_copy(turn).wait_recv()
            mixed = mix(state, lead_w.at[turn])
            if arriving:
                pl.when(jnp.logical_not(both(is_last_pos, turn == 1)))(g_arrival(turn).wait_recv)
            cur[...] = state + coarse_size * mixed + defects[turn]
            return carry

        lax.fori_loop(low, high, step, 0)

    def extra_step(q):
        state = cur[...]
        for index in halves:
            cross_copy(index).wait_recv()
        mixed = mix(state, lead_w.at[extra])
        g_arrival(q).wait_recv()
        cur[...] = state + coarse_size * mixed + defects[q]

    half_planes = size_x // 2
    direct = [(0, 0), (0, 1), (2, 0), (2, 1), (1, 1)]
    targets = (last - core, last - span - core, core)

    def top_copy(p, h):
        planes = pl.ds(h * half_planes, half_planes)
        return remote(top_out.at[planes], top_in.at[planes], top_send.at[p, h], top_recv.at[h], device(targets[p], 1))

    def top_relay():
        planes = pl.ds(0, half_planes)
        return remote(top_in.at[planes], top_in.at[planes], relay_send.at[0], top_recv.at[0], device(pos - span))

    def top_side(h):
        planes = pl.ds(h * half_planes, half_planes)
        return remote(top_in.at[planes], top_in.at[planes], relay_send.at[h + 1], top_recv.at[h],
                      device(2 * last - 1 - pos))

    is_primary = both(later, pos == last - core)

    def send_top():
        for p, h in direct:
            top_copy(p, h).start()

    start_copy = remote(c_point, start_in, start_send, start_recv, device(last, 1))

    @pl.when(both(opening, is_upper))
    def _():
        seed_copy(0).wait_recv()
        cur[...] = seed_in[...]

        @pl.when(both(is_last_pos, finishes))
        def _():
            extra_step(last - 1)

        after = own_step()
        states_ref[last, 0] = after
        cur[...] = after

        @pl.when(both(pos == last - 1, finishes))
        def _():
            seed_out[...] = after
            seed_copy(last).start()
            extra_step(last)

        @pl.when(both(finishes, has_group_after))
        def _():
            top_out[...] = cur[...]
            send_top()

    relaxes = both(later, pos == 0)
    point_copy = remote(c_point, seed_in, origin_send, seed_recv, device(last))

    @pl.when(relaxes)
    def _():
        def step(turn, carry):
            state = cur[...]
            sib_copy(turn - 1).wait_recv()
            mixed = mix(state, lead_w.at[turn - 1])

            @pl.when(turn == last - 1)
            def _():
                y_copy(last - 1).wait_recv()
                sib_copy(last - 1).start()

            after = state + coarse_size * mixed

            @pl.when(turn < last)
            def _():
                g_arrival(turn).wait_recv()
                cur[...] = after + defects[turn]

            @pl.when(turn == last)
            def _():
                c_point[...] = after

            return carry

        lax.fori_loop(1, COARSEN, step, 0)
        point_copy.start()

    @pl.when(both(ends_later, has_group_after))
    def _():
        point_copy.wait_recv()
        c_point[...] = seed_in[...] + defects[last]
        start_copy.start()

    has_start = both(is_last_pos, group > 1)

    @pl.when(has_start)
    def _():
        start_copy.wait_recv()
        g_arrival(1).wait_recv()
        g_turn.start()
        cur[...] = start_in[...]
        chain(0, last, arriving=True)
        corner = own_step()
        residual_ref[0, 0] = corner
        start = start_in[...]
        top_out[...] = corner - start - top_size * mix(start, own_w)

    @pl.when(later)
    def _():
        @pl.when(both(jnp.logical_not(is_primary), both(is_last_pos, jnp.logical_not(has_start))))
        def _():
            g_arrival(1).wait_recv()
            g_turn.start()

        top_copy(0, 0).wait_recv()
        pl.when(is_primary)(lambda: (top_side(0).start(), top_relay().start(), None)[-1])
        top_copy(0, 1).wait_recv()
        pl.when(is_primary)(lambda: top_side(1).start())

        @pl.when(both(is_primary, both(is_last_pos, jnp.logical_not(has_start))))
        def _():
            g_arrival(1).wait_recv()
            g_turn.start()

    @pl.when(has_start)
    def _():
        solved = top_in[...]
        top_out[...] = solved + top_size * mix(solved, own_w) + top_out[...]
        pl.when(has_group_after)(send_top)

    @pl.when(later)
    def _():
        cur[...] = top_in[...]
        pl.when(has_start)(lambda: chain(0, last))
        pl.when(jnp.logical_not(has_start))(lambda: chain(0, pos, arriving=True))
        after = own_step()
        states_ref[last, 0] = jnp.where(has_start, top_out[...], after)

        @pl.when(jnp.logical_not(has_start))
        def _():
            residual_ref[0, 0] = after

        @pl.when(both(both(is_last_pos, group == 1), has_group_after))
        def _():
            top_out[...] = after
            send_top()

    @pl.when(opening)
    def _():
        residual_ref[0, 0] = states_ref[last, 0]

    @pl.when(me > 1)
    def _():
        cur[...] = head[...] + fine_size * (head_mix[...] + bias_ref[0])
        states_ref[0, 0] = cur[...]

        def last_sweep(layer, carry):
            after = fine_step(layer)[2]
            cur[...] = after
            states_ref[layer, 0] = after
            return carry

        lax.fori_loop(1, depth - 1, last_sweep, 0)

    @pl.when(both(ends_later, jnp.logical_not(has_group_after)))
    def _():
        point_copy.wait_recv()

    corner = residual_ref[0, 0]
    residual_ref[0, 0] = corner - jnp.where(ends_later, seed_in[...] + defects[last], corner)

    hands_on = both(both(opening, pos == 1), core == 0)

    @pl.when(both(both(opening, pos == 1), core == 1))
    def _():
        seed_copy(last - 1).wait_send()
        open_gate(1)

    @pl.when(hands_on)
    def _():
        pl.semaphore_wait(gate.at[1], 1)
        seed_copy(last - 1).start()

    pl.when(both(has_next, jnp.logical_not(leads)))(first_hop.wait_send)
    pl.when(has_next)(second_hop.wait_send)
    for p in range(1, COARSEN):
        sends_w = both(pos > 0, pos < last) if p == last else pos < 1
        pl.when(both(later, sends_w))(w_copy(p).wait_send)
        pl.when(gives_g(p))(g_copy(p).wait_send)
    pl.when(gives_seed(last))(seed_copy(last).wait_send)
    pl.when(hands_on)(seed_copy(last - 1).wait_send)
    for q in range(last):
        pl.when(holds(q))(y_copy(q).wait_send)
        pl.when(holds(q))(sib_copy(q).wait_send)

    @pl.when(ends_later)
    def _():
        w_turn.wait_send()
        g_turn.wait_send()

    @pl.when(gives_extra)
    def _():
        for index in halves:
            extra_copy(index).wait_send()

    @pl.when(finishes)
    def _():
        for index in halves:
            cross_copy(index).wait_send()

    @pl.when(both(has_group_after, either(finishes, ends_later)))
    def _():
        for p, h in direct:
            top_copy(p, h).wait_send()

    @pl.when(is_primary)
    def _():
        top_relay().wait_send()
        top_side(0).wait_send()
        top_side(1).wait_send()

    pl.when(both(later, pos == 1))(w_ahead.wait_send)

    @pl.when(both(later, pos > 0))
    def _():
        w_back.wait_send()
        pl.when(pos < last)(g_back.wait_send)

    @pl.when(relaxes)
    def _():
        point_copy.wait_send()

    pl.when(both(ends_later, has_group_after))(start_copy.wait_send)


def shards(inputs, guess_states, kernels, biases):
    sections = lax.axis_size("layer")
    depth = guess_states.shape[0]
    state = inputs.shape[1:]
    width = state[-1]
    rows = TAPS * TAPS * width
    vmem = pl.BlockSpec(memory_space=pltpu.VMEM)
    hbm = pl.BlockSpec(memory_space=pltpu.HBM)
    kernel_rows = kernels.reshape(depth, TAPS, rows, width)
    bias_rows = biases.reshape(depth, 1, 1, width)
    f32_state = pltpu.VMEM(state, jnp.float32)
    dma = pltpu.SemaphoreType.DMA
    operands = [pltpu.with_memory_space_constraint(operand, pltpu.HBM)
                for operand in (inputs.reshape(state), guess_states, kernel_rows, bias_rows)]

    def body(*refs):
        cycle_kernel(sections, *refs)

    kept = pl.pallas_call(
        body,
        name="mgrit_cycle",
        out_shape=(
            pltpu.VMEM(guess_states.shape, jnp.float32),
            pltpu.VMEM((1,) + guess_states.shape[1:], jnp.float32),
        ),
        in_specs=[hbm, hbm, hbm, hbm],
        out_specs=(vmem, vmem),
        scratch_shapes=[
            f32_state, pltpu.VMEM(bias_rows.shape, jnp.float32),
            pltpu.VMEM((rows, TAPS * width), jnp.bfloat16),
            pltpu.VMEM((depth - 1, rows + 2 * TAPS * width, 2 * width), jnp.bfloat16),
            pltpu.VMEM((COARSEN - 1, rows, TAPS * width), jnp.bfloat16),
            pltpu.VMEM((state[0], state[1] * state[2], rows), jnp.bfloat16),
            f32_state, f32_state, f32_state, f32_state, f32_state, f32_state,
            f32_state, f32_state, f32_state, f32_state, f32_state, f32_state,
            pltpu.VMEM((COARSEN,) + state, jnp.float32),
            dma((TAPS,)), dma((depth - 1, TAPS + 1)), dma((2,)), dma((2,)), dma((2,)),
            dma((COARSEN,)), dma((COARSEN - 1,)), dma((COARSEN - 1,)), dma((COARSEN - 1,)),
            dma((COARSEN - 1,)), dma((COARSEN - 1,)), dma((PIECES // 2,)), dma((PIECES // 2,)),
            dma((PIECES // 2,)), dma((PIECES // 2,)), pltpu.SemaphoreType.REGULAR((2,)),
            dma((COARSEN,)), dma((COARSEN,)), dma((COARSEN,)), dma, dma, dma, dma,
            dma((3, 2)), dma((2,)), dma((3,)), dma((2,)), dma((2,)), dma,
        ],
        compiler_params=pltpu.CompilerParams(
            collective_id=0, has_side_effects=True, vmem_limit_bytes=24 * 1024 * 1024),
    )(*operands)

    def flush(states_ref, residual_ref, states_out, residual_out, sem):
        copies = [pltpu.make_async_copy(source, target, sem.at[index])
                  for index, (source, target) in enumerate(((states_ref, states_out), (residual_ref, residual_out)))]
        for copy in copies:
            copy.start()
        for copy in copies:
            copy.wait()

    return tuple(pl.pallas_call(
        flush,
        name="flush",
        out_shape=tuple(jax.ShapeDtypeStruct(array.shape, jnp.float32) for array in kept),
        in_specs=[vmem, vmem],
        out_specs=(hbm, hbm),
        scratch_shapes=[dma((2,))],
        compiler_params=pltpu.CompilerParams(vmem_limit_bytes=4 * 1024 * 1024),
    )(*[pltpu.with_memory_space_constraint(array, pltpu.VMEM) for array in kept]))


def solution(mesh):
    return jax.shard_map(
        shards,
        mesh=mesh,
        in_specs=(
            P("batch", None, None, None, None),
            P("layer", "batch", None, None, None, None),
            P("layer", None, None, None, None, None),
            P("layer", None),
        ),
        out_specs=(
            P("layer", "batch", None, None, None, None),
            P("layer", "batch", None, None, None, None),
        ),
        check_vma=False,
    )
```

```python
import jax
import jax.numpy as jnp
from jax import lax
from jax.experimental import pallas as pl
from jax.experimental.pallas import tpu as pltpu
from jax.sharding import PartitionSpec as P

COARSEN = 4
TAPS = 3
PIECES = 4
MESH = pl.DeviceIdType.MESH


def cycle_kernel(sections, inputs_hbm, guess_ref, kern_ref, bias_hbm, states_ref, residual_ref,
                 inputs_ref, bias_ref, own_w, fine_w, lead_w, patches, cur, head, head_mix,
                 first_head, next_head, corner_out, seed_out, seed_in, c_point,
                 start_in, top_in, top_out, defects,
                 own_sem, load_sem, small_sem, hop_send, hop_recv, w_send, w_recv, y_send, y_recv, sib_send, sib_recv,
                 extra_send, extra_recv, cross_send, cross_recv, gate,
                 g_send, g_recv, seed_send, seed_recv, origin_send, start_send, start_recv, top_send, top_recv, relay_send, turn_send, back_send, ahead_send):
    depth = guess_ref.shape[0]
    size_x, size_y, size_z, width = inputs_ref.shape
    groups = sections // COARSEN
    fine_size = 2.0 / (depth * sections)
    coarse_size = depth * fine_size
    top_size = COARSEN * coarse_size
    rows = TAPS * TAPS * width
    piece_rows = rows // PIECES
    tap_rows = TAPS * width
    far_rows = 2 * tap_rows
    last = COARSEN - 1
    extra = COARSEN - 2
    span = COARSEN // 2
    me = lax.axis_index("layer")
    part = lax.axis_index("batch")
    pos = lax.rem(me, COARSEN)
    group = me // COARSEN
    core = lax.rem(part, 2)
    row = lax.rem(part // 2, 2)
    sibling = part + 1 - 2 * core
    across = part + 2 - 4 * row
    both = jnp.logical_and
    either = jnp.logical_or
    is_first = me == 0
    has_next = me < sections - 1
    later = group > 0
    opening = group == 0
    has_group_after = group < groups - 1
    is_last_pos = pos == last
    is_upper = pos >= last - 1

    def device(p, ahead=0):
        return ((group + ahead) * COARSEN + p, part)

    barrier = pltpu.get_barrier_semaphore()

    def greet(target):
        pl.semaphore_signal(barrier, inc=1, device_id=target, device_id_type=MESH)

    for rel in range(1, COARSEN):
        greet(device(lax.rem(pos + rel, COARSEN)))
    greet((me, sibling))
    greet((me, across))
    greets_ahead = both(is_upper, has_group_after)

    @pl.when(greets_ahead)
    def _():
        for p in range(COARSEN):
            greet(device(p, 1))

    @pl.when(later)
    def _():
        for p in (last - 1, last):
            greet(device(p, -1))

    def own_load(tap):
        return pltpu.make_async_copy(
            kern_ref.at[0, tap], own_w.at[:, pl.ds(tap * width, width)], own_sem.at[tap])

    parts = ((0, 0, rows, 0, 0), (1, 0, rows, 0, width),
             (2, 0, far_rows, rows, 0), (2, far_rows, tap_rows, rows + tap_rows, width))

    def fine_load(layer, index):
        tap, start, count, place, column = parts[index]
        return pltpu.make_async_copy(
            kern_ref.at[layer, tap, pl.ds(start, count)],
            fine_w.at[layer - 1, pl.ds(place, count), pl.ds(column, width)],
            load_sem.at[layer - 1, index],
        )

    inputs_load = pltpu.make_async_copy(inputs_hbm, inputs_ref, small_sem.at[0])
    bias_load = pltpu.make_async_copy(bias_hbm, bias_ref, small_sem.at[1])
    inputs_load.start()
    bias_load.start()
    for tap in range(TAPS):
        own_load(tap).start()
    for layer in range(1, depth):
        for index in range(len(parts)):
            fine_load(layer, index).start()
    fine_w[:, rows:rows + tap_rows, width:] = jnp.zeros((depth - 1, tap_rows, width), jnp.bfloat16)

    greetings = COARSEN + 1 + jnp.where(greets_ahead, COARSEN, 0) + jnp.where(later, 2, 0)
    pl.semaphore_wait(barrier, greetings)

    def remote(source, target, send_sem, recv_sem, where):
        return pltpu.make_async_remote_copy(
            src_ref=source, dst_ref=target, send_sem=send_sem, recv_sem=recv_sem,
            device_id=where, device_id_type=MESH)

    def hop(index, source, target):
        return remote(source, target, hop_send.at[index], hop_recv.at[index], (me + 1, part))

    first_hop = hop(0, guess_ref.at[depth - 1, 0], first_head)
    second_hop = hop(1, corner_out, next_head)
    staggers = both(has_next, me < 2)
    leads = both(staggers, core == jnp.where(me == 1, 1, 0))
    trails = both(staggers, jnp.logical_not(leads))
    waits_loads = both(core == 1, me > 1)
    pl.when(both(has_next, jnp.logical_not(either(trails, waits_loads))))(first_hop.start)

    def open_gate(index):
        pl.semaphore_signal(gate.at[index], inc=1, device_id=(me, sibling), device_id_type=MESH)


    slot = jnp.minimum(pos, last - 1)
    quarter = pl.ds(pl.multiple_of((core * 2 + row) * piece_rows, 16), piece_rows)
    half = pl.ds(pl.multiple_of(core * 2 * piece_rows, 16), 2 * piece_rows)

    def w_copy(p):
        return remote(own_w.at[quarter], lead_w.at[slot, quarter], w_send.at[p], w_recv.at[slot], device(p))

    def w_arrival(q):
        return remote(lead_w.at[q, quarter], lead_w.at[q, quarter], w_send.at[0], w_recv.at[q], device(q))

    w_turn = remote(lead_w.at[1, quarter], lead_w.at[1, quarter], turn_send.at[0], w_recv.at[1], device(last - 1))

    def y_copy(q):
        return remote(lead_w.at[q, quarter], lead_w.at[q, quarter], y_send.at[q], y_recv.at[q], (me, across))

    def sib_copy(q):
        return remote(lead_w.at[q, half], lead_w.at[q, half], sib_send.at[q], sib_recv.at[q], (me, sibling))

    def extra_copy(index):
        piece = pl.ds(pl.multiple_of((row * 2 + index) * piece_rows, 16), piece_rows)
        return remote(own_w.at[piece], lead_w.at[extra, piece], extra_send.at[index], extra_recv.at[index],
                      device(2 * last - 1 - pos))

    def cross_copy(index):
        piece = pl.ds(pl.multiple_of((row * 2 + index) * piece_rows, 16), piece_rows)
        return remote(lead_w.at[extra, piece], lead_w.at[extra, piece], cross_send.at[index], cross_recv.at[index],
                      (me, across))

    gives_extra = both(opening, either(both(pos == last - 1, core == 0), both(pos == last, core == 1)))
    finishes = both(opening, either(both(pos == last, core == 0), both(pos == last - 1, core == 1)))

    def send_w(source, targets):
        @pl.when(both(later, pos == source))
        def _():
            for p in targets:
                w_copy(p).start()

    halves = range(PIECES // 2)

    def send_extra(source):
        @pl.when(both(gives_extra, pos == source))
        def _():
            for index in halves:
                extra_copy(index).start()

    def pass_extra(target):
        @pl.when(both(finishes, pos == target))
        def _():
            for index in halves:
                extra_copy(index).wait_recv()
                cross_copy(index).start()

    w_ahead = remote(lead_w.at[0, quarter], lead_w.at[0, quarter], ahead_send, w_recv.at[0], device(last))
    back_slot = jnp.maximum(pos - 1, 0)
    w_back = remote(own_w.at[quarter], lead_w.at[back_slot, quarter], back_send.at[0], w_recv.at[back_slot], device(0))

    def send_back(sources):
        for source in sources:
            pl.when(both(later, pos == source))(w_back.start)

    def holds(q):
        return both(later, either(pos > q, pos == 0))

    def first_wave():
        send_w(0, (2, 1))
        send_w(1, (3,))
        send_w(2, (3,))
        send_back((1, 2))

    def pass_w(target, qs):
        @pl.when(both(later, pos == target))
        def _():
            for q in qs:
                w_arrival(q).wait_recv()
                y_copy(q).start()
                if target == last and q == 1:
                    w_turn.start()

    for tap in range(TAPS):
        own_load(tap).wait()
    pl.when(both(has_next, waits_loads))(first_hop.start)
    send_extra(last - 1)
    inputs_load.wait()
    bias_load.wait()
    for layer in range(1, depth):
        for index in range(len(parts)):
            fine_load(layer, index).wait()
    send_extra(last)

    def let_pass():
        first_hop.wait_send()
        open_gate(0)

    def follow():
        pl.semaphore_wait(gate.at[0], 1)
        first_hop.start()

    first_wave()
    pl.when(both(leads, me > 0))(let_pass)
    pl.when(both(trails, me > 0))(follow)

    z_index = lax.broadcasted_iota(jnp.int32, (size_x * size_y, size_z, width), 1)

    def gather(state):
        squashed = jnp.tanh(state).reshape(size_x * size_y, size_z, width)
        below = jnp.where(z_index == 0, 0.0, pltpu.roll(squashed, 1, 1))
        above = jnp.where(z_index == size_z - 1, 0.0, pltpu.roll(squashed, size_z - 1, 1))
        span = size_y * size_z
        edge = jnp.zeros((size_x, size_z, width), jnp.float32)
        for tap_z, shifted in enumerate((below, squashed, above)):
            shifted = shifted.reshape(size_x, span, width)
            even = shifted.astype(jnp.bfloat16)
            odd = jnp.concatenate([edge, shifted, edge], 1).astype(jnp.bfloat16)
            for tap_y, block in enumerate((odd[:, :span], even, odd[:, 2 * size_z:])):
                column = (tap_y * TAPS + tap_z) * width
                patches[:, :, column:column + width] = block
        return patches[...].reshape(size_x * span, rows)

    def mix(state, weights):
        left = gather(state)
        product = jnp.dot(left, weights[...], preferred_element_type=jnp.float32)
        product = product.reshape(size_x, size_y, size_z, TAPS * width)
        plane = jnp.zeros((1, size_y, size_z, width), jnp.float32)
        total = product[..., width:2 * width]
        total = total + jnp.concatenate([plane, product[:-1, :, :, :width]], 0)
        return total + jnp.concatenate([product[1:, :, :, 2 * width:], plane], 0)

    def packed_mix(state, weights):
        left = gather(state)
        near = jnp.dot(left, weights[:rows], preferred_element_type=jnp.float32)
        far = jnp.dot(left[:, :far_rows], weights[rows:], preferred_element_type=jnp.float32)
        near = near.reshape(size_x, size_y, size_z, 2 * width)
        far = far.reshape(size_x, size_y, size_z, 2 * width)
        plane = jnp.zeros((1, size_y, size_z, width), jnp.float32)
        line = jnp.zeros((size_x - 1, 1, size_z, width), jnp.float32)
        ahead = far[1:, :, :, :width] + jnp.concatenate([far[1:, 1:, :, width:], line], 1)
        total = near[..., width:]
        total = total + jnp.concatenate([plane, near[:-1, :, :, :width]], 0)
        return total + jnp.concatenate([ahead, plane], 0)

    def fine_step(layer, lead=False):
        state = cur[...]
        mixed = mix(state, own_w) if lead else packed_mix(state, fine_w.at[layer - 1])
        return state, mixed, state + fine_size * (mixed + bias_ref[layer])

    pl.when(me > 0)(first_hop.wait_recv)
    cur[...] = jnp.where(is_first, inputs_ref[...], first_head[...])

    def sweep_one(layer, carry, lead=False):
        after = fine_step(layer, lead)[2]
        cur[...] = after
        states_ref[layer, 0] = after
        pl.when(both(both(leads, is_first), layer == depth - 2))(let_pass)
        pl.when(both(both(trails, is_first), layer == depth - 2))(follow)
        return carry

    sweep_one(0, 0, True)
    lax.fori_loop(1, depth, sweep_one, 0)
    corner_out[...] = cur[...]
    pl.when(has_next)(second_hop.start)
    pass_extra(last)
    pass_extra(last - 1)
    pass_w(0, (1, 0))
    pass_w(1, (0,))
    pass_w(2, (0,))
    pass_w(3, (1, 2))

    def seed_copy(p):
        return remote(seed_out, seed_in, seed_send.at[p], seed_recv, device(p))

    def gives_seed(p):
        exact = both(opening, pos == 1)
        if p == last:
            handed = both(opening, both(pos == 2, core == 1))
            return either(both(exact, core == 0), handed)
        return exact

    takes_seed = either(is_last_pos, both(opening, pos == last - 1))

    def g_copy(p):
        return remote(defects.at[pos], defects.at[pos], g_send.at[p], g_recv.at[pos], device(p))

    def g_arrival(q):
        return remote(defects.at[q], defects.at[q], g_send.at[0], g_recv.at[q], device(q))

    def gives_g(p):
        if p == last:
            return both(pos < p, either(later, both(pos == last - 1, core == 0)))
        ahead = both(pos < (1 if p == last - 1 else p), later)
        return either(ahead, both(opening, both(is_last_pos, core == 1))) if p == last - 1 else ahead

    @pl.when(me > 0)
    def _():
        second_hop.wait_recv()
        pl.when(both(later, pos == 1))(w_ahead.start)
        send_back((3,))
        head[...] = next_head[...]
        cur[...] = next_head[...]

        def sweep_two(layer, carry, lead=False):
            _, mixed, after = fine_step(layer, lead)
            if lead:
                head_mix[...] = mixed
            cur[...] = after
            states_ref[layer, 0] = after
            return carry

        sweep_two(0, 0, True)
        lax.fori_loop(1, depth, sweep_two, 0)

        @pl.when(opening)
        def _():
            seed_out[...] = cur[...]
            pl.when(both(gives_seed(last), pos == 1))(seed_copy(last).start)
            pl.when(both(gives_seed(last - 1), core == 1))(seed_copy(last - 1).start)

        defects[pos] = cur[...] - head[...] - coarse_size * head_mix[...]
        for p in (last, last - 1, 1):
            pl.when(gives_g(p))(g_copy(p).start)

    g_turn = remote(defects.at[1], defects.at[1], turn_send.at[1], g_recv.at[1], device(last - 1))

    g_back = remote(defects.at[pos], defects.at[pos], back_send.at[1], g_recv.at[pos], device(0))
    pl.when(both(later, both(pos > 0, pos < last)))(g_back.start)
    pass_w(2, (1,))
    pass_w(3, (0,))


    for q in range(last):
        @pl.when(both(later, either(pos > q, both(pos == 0, q < last - 1))))
        def _(q=q):
            y_copy(q).wait_recv()
            sib_copy(q).start()

    pass_w(0, (2,))

    ends_later = both(is_last_pos, later)
    def own_step():
        state = cur[...]
        mixed = mix(state, own_w)
        head[...] = state
        head_mix[...] = mixed
        return state + coarse_size * mixed + defects[pos]

    def chain(low, high, arriving=False):
        def step(turn, carry):
            state = cur[...]
            if arriving:
                sib_copy(turn).wait_recv()
            mixed = mix(state, lead_w.at[turn])
            if arriving:
                pl.when(jnp.logical_not(both(is_last_pos, turn == 1)))(g_arrival(turn).wait_recv)
            cur[...] = state + coarse_size * mixed + defects[turn]
            return carry

        lax.fori_loop(low, high, step, 0)

    def extra_step(q):
        state = cur[...]
        for index in halves:
            cross_copy(index).wait_recv()
        mixed = mix(state, lead_w.at[extra])
        g_arrival(q).wait_recv()
        cur[...] = state + coarse_size * mixed + defects[q]

    half_planes = size_x // 2
    direct = [(0, 0), (0, 1), (2, 0), (2, 1), (1, 1)]
    targets = (last - core, last - span - core, core)

    def top_copy(p, h):
        planes = pl.ds(h * half_planes, half_planes)
        return remote(top_out.at[planes], top_in.at[planes], top_send.at[p, h], top_recv.at[h], device(targets[p], 1))

    def top_relay():
        planes = pl.ds(0, half_planes)
        return remote(top_in.at[planes], top_in.at[planes], relay_send.at[0], top_recv.at[0], device(pos - span))

    def top_side(h):
        planes = pl.ds(h * half_planes, half_planes)
        return remote(top_in.at[planes], top_in.at[planes], relay_send.at[h + 1], top_recv.at[h],
                      device(2 * last - 1 - pos))

    is_primary = both(later, pos == last - core)

    def send_top():
        for p, h in direct:
            top_copy(p, h).start()

    start_copy = remote(c_point, start_in, start_send, start_recv, device(last, 1))

    @pl.when(both(opening, is_upper))
    def _():
        seed_copy(0).wait_recv()
        cur[...] = seed_in[...]

        @pl.when(both(is_last_pos, finishes))
        def _():
            extra_step(last - 1)

        after = own_step()
        states_ref[last, 0] = after
        cur[...] = after

        @pl.when(both(pos == last - 1, finishes))
        def _():
            seed_out[...] = after
            seed_copy(last).start()
            extra_step(last)

        @pl.when(both(finishes, has_group_after))
        def _():
            top_out[...] = cur[...]
            send_top()

    relaxes = both(later, pos == 0)
    point_copy = remote(c_point, seed_in, origin_send, seed_recv, device(last))

    @pl.when(relaxes)
    def _():
        def step(turn, carry):
            state = cur[...]
            sib_copy(turn - 1).wait_recv()
            mixed = mix(state, lead_w.at[turn - 1])

            @pl.when(turn == last - 1)
            def _():
                y_copy(last - 1).wait_recv()
                sib_copy(last - 1).start()

            after = state + coarse_size * mixed

            @pl.when(turn < last)
            def _():
                g_arrival(turn).wait_recv()
                cur[...] = after + defects[turn]

            @pl.when(turn == last)
            def _():
                c_point[...] = after

            return carry

        lax.fori_loop(1, COARSEN, step, 0)
        point_copy.start()

    @pl.when(both(ends_later, has_group_after))
    def _():
        point_copy.wait_recv()
        c_point[...] = seed_in[...] + defects[last]
        start_copy.start()

    has_start = both(is_last_pos, group > 1)

    @pl.when(has_start)
    def _():
        start_copy.wait_recv()
        g_arrival(1).wait_recv()
        g_turn.start()
        cur[...] = start_in[...]
        chain(0, last, arriving=True)
        corner = own_step()
        residual_ref[0, 0] = corner
        start = start_in[...]
        top_out[...] = corner - start - top_size * mix(start, own_w)

    @pl.when(later)
    def _():
        @pl.when(both(jnp.logical_not(is_primary), both(is_last_pos, jnp.logical_not(has_start))))
        def _():
            g_arrival(1).wait_recv()
            g_turn.start()

        top_copy(0, 0).wait_recv()
        pl.when(is_primary)(lambda: (top_side(0).start(), top_relay().start(), None)[-1])
        top_copy(0, 1).wait_recv()
        pl.when(is_primary)(lambda: top_side(1).start())

        @pl.when(both(is_primary, both(is_last_pos, jnp.logical_not(has_start))))
        def _():
            g_arrival(1).wait_recv()
            g_turn.start()

    @pl.when(has_start)
    def _():
        solved = top_in[...]
        top_out[...] = solved + top_size * mix(solved, own_w) + top_out[...]
        pl.when(has_group_after)(send_top)

    @pl.when(later)
    def _():
        cur[...] = top_in[...]
        pl.when(has_start)(lambda: chain(0, last))
        pl.when(jnp.logical_not(has_start))(lambda: chain(0, pos, arriving=True))
        after = own_step()
        states_ref[last, 0] = jnp.where(has_start, top_out[...], after)

        @pl.when(jnp.logical_not(has_start))
        def _():
            residual_ref[0, 0] = after

        @pl.when(both(both(is_last_pos, group == 1), has_group_after))
        def _():
            top_out[...] = after
            send_top()

    @pl.when(opening)
    def _():
        residual_ref[0, 0] = states_ref[last, 0]

    @pl.when(me > 1)
    def _():
        cur[...] = head[...] + fine_size * (head_mix[...] + bias_ref[0])
        states_ref[0, 0] = cur[...]

        def last_sweep(layer, carry):
            after = fine_step(layer)[2]
            cur[...] = after
            states_ref[layer, 0] = after
            return carry

        lax.fori_loop(1, depth - 1, last_sweep, 0)

    @pl.when(both(ends_later, jnp.logical_not(has_group_after)))
    def _():
        point_copy.wait_recv()

    corner = residual_ref[0, 0]
    residual_ref[0, 0] = corner - jnp.where(ends_later, seed_in[...] + defects[last], corner)

    hands_on = both(both(opening, pos == 1), core == 0)

    @pl.when(both(both(opening, pos == 1), core == 1))
    def _():
        seed_copy(last - 1).wait_send()
        open_gate(1)

    @pl.when(hands_on)
    def _():
        pl.semaphore_wait(gate.at[1], 1)
        seed_copy(last - 1).start()

    pl.when(both(has_next, jnp.logical_not(leads)))(first_hop.wait_send)
    pl.when(has_next)(second_hop.wait_send)
    for p in range(1, COARSEN):
        sends_w = both(pos > 0, pos < last) if p == last else pos < 1
        pl.when(both(later, sends_w))(w_copy(p).wait_send)
        pl.when(gives_g(p))(g_copy(p).wait_send)
    pl.when(gives_seed(last))(seed_copy(last).wait_send)
    pl.when(hands_on)(seed_copy(last - 1).wait_send)
    for q in range(last):
        pl.when(holds(q))(y_copy(q).wait_send)
        pl.when(holds(q))(sib_copy(q).wait_send)

    @pl.when(ends_later)
    def _():
        w_turn.wait_send()
        g_turn.wait_send()

    @pl.when(gives_extra)
    def _():
        for index in halves:
            extra_copy(index).wait_send()

    @pl.when(finishes)
    def _():
        for index in halves:
            cross_copy(index).wait_send()

    @pl.when(both(has_group_after, either(finishes, ends_later)))
    def _():
        for p, h in direct:
            top_copy(p, h).wait_send()

    @pl.when(is_primary)
    def _():
        top_relay().wait_send()
        top_side(0).wait_send()
        top_side(1).wait_send()

    pl.when(both(later, pos == 1))(w_ahead.wait_send)

    @pl.when(both(later, pos > 0))
    def _():
        w_back.wait_send()
        pl.when(pos < last)(g_back.wait_send)

    @pl.when(relaxes)
    def _():
        point_copy.wait_send()

    pl.when(both(ends_later, has_group_after))(start_copy.wait_send)


def shards(inputs, guess_states, kernels, biases):
    sections = lax.axis_size("layer")
    depth = guess_states.shape[0]
    state = inputs.shape[1:]
    width = state[-1]
    rows = TAPS * TAPS * width
    vmem = pl.BlockSpec(memory_space=pltpu.VMEM)
    hbm = pl.BlockSpec(memory_space=pltpu.HBM)
    kernel_rows = kernels.reshape(depth, TAPS, rows, width)
    bias_rows = biases.reshape(depth, 1, 1, width)
    f32_state = pltpu.VMEM(state, jnp.float32)
    dma = pltpu.SemaphoreType.DMA
    operands = [pltpu.with_memory_space_constraint(operand, pltpu.HBM)
                for operand in (inputs.reshape(state), guess_states, kernel_rows, bias_rows)]

    def body(*refs):
        cycle_kernel(sections, *refs)

    kept = pl.pallas_call(
        body,
        name="mgrit_cycle",
        out_shape=(
            pltpu.VMEM(guess_states.shape, jnp.float32),
            pltpu.VMEM((1,) + guess_states.shape[1:], jnp.float32),
        ),
        in_specs=[hbm, hbm, hbm, hbm],
        out_specs=(vmem, vmem),
        scratch_shapes=[
            f32_state, pltpu.VMEM(bias_rows.shape, jnp.float32),
            pltpu.VMEM((rows, TAPS * width), jnp.bfloat16),
            pltpu.VMEM((depth - 1, rows + 2 * TAPS * width, 2 * width), jnp.bfloat16),
            pltpu.VMEM((COARSEN - 1, rows, TAPS * width), jnp.bfloat16),
            pltpu.VMEM((state[0], state[1] * state[2], rows), jnp.bfloat16),
            f32_state, f32_state, f32_state, f32_state, f32_state, f32_state,
            f32_state, f32_state, f32_state, f32_state, f32_state, f32_state,
            pltpu.VMEM((COARSEN,) + state, jnp.float32),
            dma((TAPS,)), dma((depth - 1, TAPS + 1)), dma((2,)), dma((2,)), dma((2,)),
            dma((COARSEN,)), dma((COARSEN - 1,)), dma((COARSEN - 1,)), dma((COARSEN - 1,)),
            dma((COARSEN - 1,)), dma((COARSEN - 1,)), dma((PIECES // 2,)), dma((PIECES // 2,)),
            dma((PIECES // 2,)), dma((PIECES // 2,)), pltpu.SemaphoreType.REGULAR((2,)),
            dma((COARSEN,)), dma((COARSEN,)), dma((COARSEN,)), dma, dma, dma, dma,
            dma((3, 2)), dma((2,)), dma((3,)), dma((2,)), dma((2,)), dma,
        ],
        compiler_params=pltpu.CompilerParams(
            collective_id=0, has_side_effects=True, vmem_limit_bytes=24 * 1024 * 1024),
    )(*operands)

    def flush(states_ref, residual_ref, states_out, residual_out, sem):
        copies = [pltpu.make_async_copy(source, target, sem.at[index])
                  for index, (source, target) in enumerate(((states_ref, states_out), (residual_ref, residual_out)))]
        for copy in copies:
            copy.start()
        for copy in copies:
            copy.wait()

    return tuple(pl.pallas_call(
        flush,
        name="flush",
        out_shape=tuple(jax.ShapeDtypeStruct(array.shape, jnp.float32) for array in kept),
        in_specs=[vmem, vmem],
        out_specs=(hbm, hbm),
        scratch_shapes=[dma((2,))],
        compiler_params=pltpu.CompilerParams(vmem_limit_bytes=4 * 1024 * 1024),
    )(*[pltpu.with_memory_space_constraint(array, pltpu.VMEM) for array in kept]))


def solution(mesh):
    return jax.shard_map(
        shards,
        mesh=mesh,
        in_specs=(
            P("batch", None, None, None, None),
            P("layer", "batch", None, None, None, None),
            P("layer", None, None, None, None, None),
            P("layer", None),
        ),
        out_specs=(
            P("layer", "batch", None, None, None, None),
            P("layer", "batch", None, None, None, None),
        ),
        check_vma=False,
    )
```

```python
import jax
import jax.numpy as jnp
from jax import lax
from jax.experimental import pallas as pl
from jax.experimental.pallas import tpu as pltpu
from jax.sharding import PartitionSpec as P

COARSEN = 4
TAPS = 3
PIECES = 4
MESH = pl.DeviceIdType.MESH


def cycle_kernel(sections, inputs_hbm, guess_ref, kern_ref, bias_hbm, states_ref, residual_ref,
                 inputs_ref, bias_ref, own_w, fine_w, lead_w, patches, cur, head, head_mix,
                 first_head, next_head, corner_out, seed_out, seed_in, c_point,
                 start_in, top_in, top_out, defects,
                 own_sem, load_sem, small_sem, hop_send, hop_recv, w_send, w_recv, y_send, y_recv, sib_send, sib_recv,
                 extra_send, extra_recv, cross_send, cross_recv, gate,
                 g_send, g_recv, seed_send, seed_recv, origin_send, start_send, start_recv, top_send, top_recv, relay_send, turn_send, back_send, ahead_send):
    depth = guess_ref.shape[0]
    size_x, size_y, size_z, width = inputs_ref.shape
    groups = sections // COARSEN
    fine_size = 2.0 / (depth * sections)
    coarse_size = depth * fine_size
    top_size = COARSEN * coarse_size
    rows = TAPS * TAPS * width
    piece_rows = rows // PIECES
    tap_rows = TAPS * width
    far_rows = 2 * tap_rows
    last = COARSEN - 1
    extra = COARSEN - 2
    span = COARSEN // 2
    me = lax.axis_index("layer")
    part = lax.axis_index("batch")
    pos = lax.rem(me, COARSEN)
    group = me // COARSEN
    core = lax.rem(part, 2)
    row = lax.rem(part // 2, 2)
    sibling = part + 1 - 2 * core
    across = part + 2 - 4 * row
    both = jnp.logical_and
    either = jnp.logical_or
    is_first = me == 0
    has_next = me < sections - 1
    later = group > 0
    opening = group == 0
    has_group_after = group < groups - 1
    is_last_pos = pos == last
    is_upper = pos >= last - 1

    def device(p, ahead=0):
        return ((group + ahead) * COARSEN + p, part)

    barrier = pltpu.get_barrier_semaphore()

    def greet(target):
        pl.semaphore_signal(barrier, inc=1, device_id=target, device_id_type=MESH)

    for rel in range(1, COARSEN):
        greet(device(lax.rem(pos + rel, COARSEN)))
    greet((me, sibling))
    greet((me, across))
    greets_ahead = both(is_upper, has_group_after)

    @pl.when(greets_ahead)
    def _():
        for p in range(COARSEN):
            greet(device(p, 1))

    @pl.when(later)
    def _():
        for p in (last - 1, last):
            greet(device(p, -1))

    def own_load(tap):
        return pltpu.make_async_copy(
            kern_ref.at[0, tap], own_w.at[:, pl.ds(tap * width, width)], own_sem.at[tap])

    parts = ((0, 0, rows, 0, 0), (1, 0, rows, 0, width),
             (2, 0, far_rows, rows, 0), (2, far_rows, tap_rows, rows + tap_rows, width))

    def fine_load(layer, index):
        tap, start, count, place, column = parts[index]
        return pltpu.make_async_copy(
            kern_ref.at[layer, tap, pl.ds(start, count)],
            fine_w.at[layer - 1, pl.ds(place, count), pl.ds(column, width)],
            load_sem.at[layer - 1, index],
        )

    inputs_load = pltpu.make_async_copy(inputs_hbm, inputs_ref, small_sem.at[0])
    bias_load = pltpu.make_async_copy(bias_hbm, bias_ref, small_sem.at[1])
    inputs_load.start()
    bias_load.start()
    for tap in range(TAPS):
        own_load(tap).start()
    for layer in range(1, depth):
        for index in range(len(parts)):
            fine_load(layer, index).start()
    fine_w[:, rows:rows + tap_rows, width:] = jnp.zeros((depth - 1, tap_rows, width), jnp.bfloat16)

    greetings = COARSEN + 1 + jnp.where(greets_ahead, COARSEN, 0) + jnp.where(later, 2, 0)
    pl.semaphore_wait(barrier, greetings)

    def remote(source, target, send_sem, recv_sem, where):
        return pltpu.make_async_remote_copy(
            src_ref=source, dst_ref=target, send_sem=send_sem, recv_sem=recv_sem,
            device_id=where, device_id_type=MESH)

    def hop(index, source, target):
        return remote(source, target, hop_send.at[index], hop_recv.at[index], (me + 1, part))

    first_hop = hop(0, guess_ref.at[depth - 1, 0], first_head)
    second_hop = hop(1, corner_out, next_head)
    staggers = both(has_next, me < 2)
    leads = both(staggers, core == jnp.where(me == 1, 1, 0))
    trails = both(staggers, jnp.logical_not(leads))
    waits_loads = both(core == 1, me > 1)
    pl.when(both(has_next, jnp.logical_not(either(trails, waits_loads))))(first_hop.start)

    def open_gate(index):
        pl.semaphore_signal(gate.at[index], inc=1, device_id=(me, sibling), device_id_type=MESH)


    slot = jnp.minimum(pos, last - 1)
    quarter = pl.ds(pl.multiple_of((core * 2 + row) * piece_rows, 16), piece_rows)
    half = pl.ds(pl.multiple_of(core * 2 * piece_rows, 16), 2 * piece_rows)

    def w_copy(p):
        return remote(own_w.at[quarter], lead_w.at[slot, quarter], w_send.at[p], w_recv.at[slot], device(p))

    def w_arrival(q):
        return remote(lead_w.at[q, quarter], lead_w.at[q, quarter], w_send.at[0], w_recv.at[q], device(q))

    w_turn = remote(lead_w.at[1, quarter], lead_w.at[1, quarter], turn_send.at[0], w_recv.at[1], device(last - 1))

    def y_copy(q):
        return remote(lead_w.at[q, quarter], lead_w.at[q, quarter], y_send.at[q], y_recv.at[q], (me, across))

    def sib_copy(q):
        return remote(lead_w.at[q, half], lead_w.at[q, half], sib_send.at[q], sib_recv.at[q], (me, sibling))

    def extra_copy(index):
        piece = pl.ds(pl.multiple_of((row * 2 + index) * piece_rows, 16), piece_rows)
        return remote(own_w.at[piece], lead_w.at[extra, piece], extra_send.at[index], extra_recv.at[index],
                      device(2 * last - 1 - pos))

    def cross_copy(index):
        piece = pl.ds(pl.multiple_of((row * 2 + index) * piece_rows, 16), piece_rows)
        return remote(lead_w.at[extra, piece], lead_w.at[extra, piece], cross_send.at[index], cross_recv.at[index],
                      (me, across))

    gives_extra = both(opening, either(both(pos == last - 1, core == 0), both(pos == last, core == 1)))
    finishes = both(opening, either(both(pos == last, core == 0), both(pos == last - 1, core == 1)))

    def send_w(source, targets):
        @pl.when(both(later, pos == source))
        def _():
            for p in targets:
                w_copy(p).start()

    halves = range(PIECES // 2)

    def send_extra(source):
        @pl.when(both(gives_extra, pos == source))
        def _():
            for index in halves:
                extra_copy(index).start()

    def pass_extra(target):
        @pl.when(both(finishes, pos == target))
        def _():
            for index in halves:
                extra_copy(index).wait_recv()
                cross_copy(index).start()

    w_ahead = remote(lead_w.at[0, quarter], lead_w.at[0, quarter], ahead_send, w_recv.at[0], device(last))
    back_slot = jnp.maximum(pos - 1, 0)
    w_back = remote(own_w.at[quarter], lead_w.at[back_slot, quarter], back_send.at[0], w_recv.at[back_slot], device(0))

    def send_back(sources):
        for source in sources:
            pl.when(both(later, pos == source))(w_back.start)

    def holds(q):
        return both(later, either(pos > q, both(pos == 0, q < last - 1)))

    def first_wave():
        send_w(0, (2, 1))
        send_w(1, (3,))
        send_w(2, (3,))
        send_back((1, 2))

    def pass_w(target, qs):
        @pl.when(both(later, pos == target))
        def _():
            for q in qs:
                w_arrival(q).wait_recv()
                y_copy(q).start()
                if target == last and q == 1:
                    w_turn.start()

    for tap in range(TAPS):
        own_load(tap).wait()
    pl.when(both(has_next, waits_loads))(first_hop.start)
    send_extra(last - 1)
    inputs_load.wait()
    bias_load.wait()
    for layer in range(1, depth):
        for index in range(len(parts)):
            fine_load(layer, index).wait()
    send_extra(last)

    def let_pass():
        first_hop.wait_send()
        open_gate(0)

    def follow():
        pl.semaphore_wait(gate.at[0], 1)
        first_hop.start()

    first_wave()
    pl.when(both(leads, me > 0))(let_pass)
    pl.when(both(trails, me > 0))(follow)

    z_index = lax.broadcasted_iota(jnp.int32, (size_x * size_y, size_z, width), 1)

    def gather(state):
        squashed = jnp.tanh(state).reshape(size_x * size_y, size_z, width)
        below = jnp.where(z_index == 0, 0.0, pltpu.roll(squashed, 1, 1))
        above = jnp.where(z_index == size_z - 1, 0.0, pltpu.roll(squashed, size_z - 1, 1))
        span = size_y * size_z
        edge = jnp.zeros((size_x, size_z, width), jnp.float32)
        for tap_z, shifted in enumerate((below, squashed, above)):
            shifted = shifted.reshape(size_x, span, width)
            even = shifted.astype(jnp.bfloat16)
            odd = jnp.concatenate([edge, shifted, edge], 1).astype(jnp.bfloat16)
            for tap_y, block in enumerate((odd[:, :span], even, odd[:, 2 * size_z:])):
                column = (tap_y * TAPS + tap_z) * width
                patches[:, :, column:column + width] = block
        return patches[...].reshape(size_x * span, rows)

    def mix(state, weights):
        left = gather(state)
        product = jnp.dot(left, weights[...], preferred_element_type=jnp.float32)
        product = product.reshape(size_x, size_y, size_z, TAPS * width)
        plane = jnp.zeros((1, size_y, size_z, width), jnp.float32)
        total = product[..., width:2 * width]
        total = total + jnp.concatenate([plane, product[:-1, :, :, :width]], 0)
        return total + jnp.concatenate([product[1:, :, :, 2 * width:], plane], 0)

    def packed_mix(state, weights):
        left = gather(state)
        near = jnp.dot(left, weights[:rows], preferred_element_type=jnp.float32)
        far = jnp.dot(left[:, :far_rows], weights[rows:], preferred_element_type=jnp.float32)
        near = near.reshape(size_x, size_y, size_z, 2 * width)
        far = far.reshape(size_x, size_y, size_z, 2 * width)
        plane = jnp.zeros((1, size_y, size_z, width), jnp.float32)
        line = jnp.zeros((size_x - 1, 1, size_z, width), jnp.float32)
        ahead = far[1:, :, :, :width] + jnp.concatenate([far[1:, 1:, :, width:], line], 1)
        total = near[..., width:]
        total = total + jnp.concatenate([plane, near[:-1, :, :, :width]], 0)
        return total + jnp.concatenate([ahead, plane], 0)

    def fine_step(layer, lead=False):
        state = cur[...]
        mixed = mix(state, own_w) if lead else packed_mix(state, fine_w.at[layer - 1])
        return state, mixed, state + fine_size * (mixed + bias_ref[layer])

    pl.when(me > 0)(first_hop.wait_recv)
    cur[...] = jnp.where(is_first, inputs_ref[...], first_head[...])

    def sweep_one(layer, carry, lead=False):
        after = fine_step(layer, lead)[2]
        cur[...] = after
        states_ref[layer, 0] = after
        pl.when(both(both(leads, is_first), layer == depth - 2))(let_pass)
        pl.when(both(both(trails, is_first), layer == depth - 2))(follow)
        return carry

    sweep_one(0, 0, True)
    lax.fori_loop(1, depth, sweep_one, 0)
    corner_out[...] = cur[...]
    pl.when(has_next)(second_hop.start)
    pass_extra(last)
    pass_extra(last - 1)
    pass_w(0, (1, 0))
    pass_w(1, (0,))
    pass_w(2, (0,))
    pass_w(3, (1, 2))

    def seed_copy(p):
        return remote(seed_out, seed_in, seed_send.at[p], seed_recv, device(p))

    def gives_seed(p):
        exact = both(opening, pos == 1)
        if p == last:
            handed = both(opening, both(pos == 2, core == 1))
            return either(both(exact, core == 0), handed)
        return exact

    takes_seed = either(is_last_pos, both(opening, pos == last - 1))

    def g_copy(p):
        return remote(defects.at[pos], defects.at[pos], g_send.at[p], g_recv.at[pos], device(p))

    def g_arrival(q):
        return remote(defects.at[q], defects.at[q], g_send.at[0], g_recv.at[q], device(q))

    def gives_g(p):
        if p == last:
            return both(pos < p, either(later, both(pos == last - 1, core == 0)))
        ahead = both(pos < (1 if p == last - 1 else p), later)
        return either(ahead, both(opening, both(is_last_pos, core == 1))) if p == last - 1 else ahead

    @pl.when(me > 0)
    def _():
        second_hop.wait_recv()
        pl.when(both(later, pos == 1))(w_ahead.start)
        head[...] = next_head[...]
        cur[...] = next_head[...]

        def sweep_two(layer, carry, lead=False):
            _, mixed, after = fine_step(layer, lead)
            if lead:
                head_mix[...] = mixed
            cur[...] = after
            states_ref[layer, 0] = after
            return carry

        sweep_two(0, 0, True)
        lax.fori_loop(1, depth, sweep_two, 0)

        @pl.when(opening)
        def _():
            seed_out[...] = cur[...]
            pl.when(both(gives_seed(last), pos == 1))(seed_copy(last).start)
            pl.when(both(gives_seed(last - 1), core == 1))(seed_copy(last - 1).start)

        defects[pos] = cur[...] - head[...] - coarse_size * head_mix[...]
        for p in (last, last - 1, 1):
            pl.when(gives_g(p))(g_copy(p).start)

    g_turn = remote(defects.at[1], defects.at[1], turn_send.at[1], g_recv.at[1], device(last - 1))

    g_back = remote(defects.at[pos], defects.at[pos], back_send.at[1], g_recv.at[pos], device(0))
    pl.when(both(later, both(pos > 0, pos < last)))(g_back.start)
    pass_w(2, (1,))
    pass_w(3, (0,))


    for q in range(last):
        @pl.when(both(later, either(pos > q, both(pos == 0, q < last - 1))))
        def _(q=q):
            y_copy(q).wait_recv()
            sib_copy(q).start()


    ends_later = both(is_last_pos, later)
    def own_step():
        state = cur[...]
        mixed = mix(state, own_w)
        head[...] = state
        head_mix[...] = mixed
        return state + coarse_size * mixed + defects[pos]

    def chain(low, high, arriving=False):
        def step(turn, carry):
            state = cur[...]
            if arriving:
                sib_copy(turn).wait_recv()
            mixed = mix(state, lead_w.at[turn])
            if arriving:
                pl.when(jnp.logical_not(both(is_last_pos, turn == 1)))(g_arrival(turn).wait_recv)
            cur[...] = state + coarse_size * mixed + defects[turn]
            return carry

        lax.fori_loop(low, high, step, 0)

    def extra_step(q):
        state = cur[...]
        for index in halves:
            cross_copy(index).wait_recv()
        mixed = mix(state, lead_w.at[extra])
        g_arrival(q).wait_recv()
        cur[...] = state + coarse_size * mixed + defects[q]

    half_planes = size_x // 2
    direct = [(0, 0), (0, 1), (2, 0), (2, 1), (1, 1)]
    targets = (last - core, last - span - core, core)

    def top_copy(p, h):
        planes = pl.ds(h * half_planes, half_planes)
        return remote(top_out.at[planes], top_in.at[planes], top_send.at[p, h], top_recv.at[h], device(targets[p], 1))

    def top_relay():
        planes = pl.ds(0, half_planes)
        return remote(top_in.at[planes], top_in.at[planes], relay_send.at[0], top_recv.at[0], device(pos - span))

    def top_side(h):
        planes = pl.ds(h * half_planes, half_planes)
        return remote(top_in.at[planes], top_in.at[planes], relay_send.at[h + 1], top_recv.at[h],
                      device(2 * last - 1 - pos))

    is_primary = both(later, pos == last - core)

    def send_top():
        for p, h in direct:
            top_copy(p, h).start()

    start_copy = remote(c_point, start_in, start_send, start_recv, device(last, 1))

    @pl.when(both(opening, is_upper))
    def _():
        seed_copy(0).wait_recv()
        cur[...] = seed_in[...]

        @pl.when(both(is_last_pos, finishes))
        def _():
            extra_step(last - 1)

        after = own_step()
        states_ref[last, 0] = after
        cur[...] = after

        @pl.when(both(pos == last - 1, finishes))
        def _():
            seed_out[...] = after
            seed_copy(last).start()
            extra_step(last)

        @pl.when(both(finishes, has_group_after))
        def _():
            top_out[...] = cur[...]
            send_top()

    relaxes = both(later, pos == 0)
    point_copy = remote(c_point, seed_in, origin_send, seed_recv, device(last))

    @pl.when(relaxes)
    def _():
        def step(turn, carry):
            state = cur[...]
            sib_copy(turn - 1).wait_recv()
            mixed = mix(state, lead_w.at[turn - 1])

            g_arrival(turn).wait_recv()
            cur[...] = state + coarse_size * mixed + defects[turn]
            return carry

        lax.fori_loop(1, last, step, 0)
        c_point[...] = cur[...]
        point_copy.start()

    @pl.when(both(ends_later, has_group_after))
    def _():
        point_copy.wait_recv()
        cur[...] = seed_in[...]
        c_point[...] = own_step()
        start_copy.start()

    has_start = both(is_last_pos, group > 1)

    @pl.when(has_start)
    def _():
        start_copy.wait_recv()
        g_arrival(1).wait_recv()
        g_turn.start()
        cur[...] = start_in[...]
        chain(0, last, arriving=True)
        corner = own_step()
        residual_ref[0, 0] = corner
        start = start_in[...]
        top_out[...] = corner - start - top_size * mix(start, own_w)

    @pl.when(later)
    def _():
        @pl.when(both(jnp.logical_not(is_primary), both(is_last_pos, jnp.logical_not(has_start))))
        def _():
            g_arrival(1).wait_recv()
            g_turn.start()

        top_copy(0, 0).wait_recv()
        pl.when(is_primary)(lambda: (top_side(0).start(), top_relay().start(), None)[-1])
        top_copy(0, 1).wait_recv()
        pl.when(is_primary)(lambda: top_side(1).start())

        @pl.when(both(is_primary, both(is_last_pos, jnp.logical_not(has_start))))
        def _():
            g_arrival(1).wait_recv()
            g_turn.start()

    @pl.when(has_start)
    def _():
        solved = top_in[...]
        top_out[...] = solved + top_size * mix(solved, own_w) + top_out[...]
        pl.when(has_group_after)(send_top)

    @pl.when(later)
    def _():
        cur[...] = top_in[...]
        pl.when(has_start)(lambda: chain(0, last))
        pl.when(jnp.logical_not(has_start))(lambda: chain(0, pos, arriving=True))
        after = own_step()
        states_ref[last, 0] = jnp.where(has_start, top_out[...], after)

        @pl.when(jnp.logical_not(has_start))
        def _():
            residual_ref[0, 0] = after

        @pl.when(both(both(is_last_pos, group == 1), has_group_after))
        def _():
            top_out[...] = after
            send_top()

    @pl.when(opening)
    def _():
        residual_ref[0, 0] = states_ref[last, 0]

    @pl.when(me > 1)
    def _():
        cur[...] = head[...] + fine_size * (head_mix[...] + bias_ref[0])
        states_ref[0, 0] = cur[...]

        def last_sweep(layer, carry):
            after = fine_step(layer)[2]
            cur[...] = after
            states_ref[layer, 0] = after
            return carry

        lax.fori_loop(1, depth - 1, last_sweep, 0)

    @pl.when(both(ends_later, jnp.logical_not(has_group_after)))
    def _():
        point_copy.wait_recv()
        cur[...] = seed_in[...]
        c_point[...] = own_step()

    corner = residual_ref[0, 0]
    residual_ref[0, 0] = corner - jnp.where(ends_later, c_point[...], corner)

    hands_on = both(both(opening, pos == 1), core == 0)

    @pl.when(both(both(opening, pos == 1), core == 1))
    def _():
        seed_copy(last - 1).wait_send()
        open_gate(1)

    @pl.when(hands_on)
    def _():
        pl.semaphore_wait(gate.at[1], 1)
        seed_copy(last - 1).start()

    pl.when(both(has_next, jnp.logical_not(leads)))(first_hop.wait_send)
    pl.when(has_next)(second_hop.wait_send)
    for p in range(1, COARSEN):
        sends_w = both(pos > 0, pos < last) if p == last else pos < 1
        pl.when(both(later, sends_w))(w_copy(p).wait_send)
        pl.when(gives_g(p))(g_copy(p).wait_send)
    pl.when(gives_seed(last))(seed_copy(last).wait_send)
    pl.when(hands_on)(seed_copy(last - 1).wait_send)
    for q in range(last):
        pl.when(holds(q))(y_copy(q).wait_send)
        pl.when(holds(q))(sib_copy(q).wait_send)

    @pl.when(ends_later)
    def _():
        w_turn.wait_send()
        g_turn.wait_send()

    @pl.when(gives_extra)
    def _():
        for index in halves:
            extra_copy(index).wait_send()

    @pl.when(finishes)
    def _():
        for index in halves:
            cross_copy(index).wait_send()

    @pl.when(both(has_group_after, either(finishes, ends_later)))
    def _():
        for p, h in direct:
            top_copy(p, h).wait_send()

    @pl.when(is_primary)
    def _():
        top_relay().wait_send()
        top_side(0).wait_send()
        top_side(1).wait_send()

    pl.when(both(later, pos == 1))(w_ahead.wait_send)

    @pl.when(both(later, pos > 0))
    def _():
        pl.when(pos < last)(w_back.wait_send)
        pl.when(pos < last)(g_back.wait_send)

    @pl.when(relaxes)
    def _():
        point_copy.wait_send()

    pl.when(both(ends_later, has_group_after))(start_copy.wait_send)


def shards(inputs, guess_states, kernels, biases):
    sections = lax.axis_size("layer")
    depth = guess_states.shape[0]
    state = inputs.shape[1:]
    width = state[-1]
    rows = TAPS * TAPS * width
    vmem = pl.BlockSpec(memory_space=pltpu.VMEM)
    hbm = pl.BlockSpec(memory_space=pltpu.HBM)
    kernel_rows = kernels.reshape(depth, TAPS, rows, width)
    bias_rows = biases.reshape(depth, 1, 1, width)
    f32_state = pltpu.VMEM(state, jnp.float32)
    dma = pltpu.SemaphoreType.DMA
    operands = [pltpu.with_memory_space_constraint(operand, pltpu.HBM)
                for operand in (inputs.reshape(state), guess_states, kernel_rows, bias_rows)]

    def body(*refs):
        cycle_kernel(sections, *refs)

    kept = pl.pallas_call(
        body,
        name="mgrit_cycle",
        out_shape=(
            pltpu.VMEM(guess_states.shape, jnp.float32),
            pltpu.VMEM((1,) + guess_states.shape[1:], jnp.float32),
        ),
        in_specs=[hbm, hbm, hbm, hbm],
        out_specs=(vmem, vmem),
        scratch_shapes=[
            f32_state, pltpu.VMEM(bias_rows.shape, jnp.float32),
            pltpu.VMEM((rows, TAPS * width), jnp.bfloat16),
            pltpu.VMEM((depth - 1, rows + 2 * TAPS * width, 2 * width), jnp.bfloat16),
            pltpu.VMEM((COARSEN - 1, rows, TAPS * width), jnp.bfloat16),
            pltpu.VMEM((state[0], state[1] * state[2], rows), jnp.bfloat16),
            f32_state, f32_state, f32_state, f32_state, f32_state, f32_state,
            f32_state, f32_state, f32_state, f32_state, f32_state, f32_state,
            pltpu.VMEM((COARSEN,) + state, jnp.float32),
            dma((TAPS,)), dma((depth - 1, TAPS + 1)), dma((2,)), dma((2,)), dma((2,)),
            dma((COARSEN,)), dma((COARSEN - 1,)), dma((COARSEN - 1,)), dma((COARSEN - 1,)),
            dma((COARSEN - 1,)), dma((COARSEN - 1,)), dma((PIECES // 2,)), dma((PIECES // 2,)),
            dma((PIECES // 2,)), dma((PIECES // 2,)), pltpu.SemaphoreType.REGULAR((2,)),
            dma((COARSEN,)), dma((COARSEN,)), dma((COARSEN,)), dma, dma, dma, dma,
            dma((3, 2)), dma((2,)), dma((3,)), dma((2,)), dma((2,)), dma,
        ],
        compiler_params=pltpu.CompilerParams(
            collective_id=0, has_side_effects=True, vmem_limit_bytes=24 * 1024 * 1024),
    )(*operands)

    def flush(states_ref, residual_ref, states_out, residual_out, sem):
        copies = [pltpu.make_async_copy(source, target, sem.at[index])
                  for index, (source, target) in enumerate(((states_ref, states_out), (residual_ref, residual_out)))]
        for copy in copies:
            copy.start()
        for copy in copies:
            copy.wait()

    return tuple(pl.pallas_call(
        flush,
        name="flush",
        out_shape=tuple(jax.ShapeDtypeStruct(array.shape, jnp.float32) for array in kept),
        in_specs=[vmem, vmem],
        out_specs=(hbm, hbm),
        scratch_shapes=[dma((2,))],
        compiler_params=pltpu.CompilerParams(vmem_limit_bytes=4 * 1024 * 1024),
    )(*[pltpu.with_memory_space_constraint(array, pltpu.VMEM) for array in kept]))


def solution(mesh):
    return jax.shard_map(
        shards,
        mesh=mesh,
        in_specs=(
            P("batch", None, None, None, None),
            P("layer", "batch", None, None, None, None),
            P("layer", None, None, None, None, None),
            P("layer", None),
        ),
        out_specs=(
            P("layer", "batch", None, None, None, None),
            P("layer", "batch", None, None, None, None),
        ),
        check_vma=False,
    )
```
